256 devices in a mesh: rows: 64 (over z, x_hi, y), cols: 4 (over x_lo, core).
Axes of the slice: x: 4 (x_hi: 2, x_lo: 2; x = x_hi * 2 + x_lo), y: 4, z: 8, core: 2. Of those that a mesh axis runs over, the one named last changes fastest.
Arguments:
- cov_panel: float32 [65536, 512], P('rows', 'cols'), may hold values from -12 to 40, as said below
- cov_slab: float32 [65536, 4096], P('rows', 'cols'), may hold values from -6 to 6
- frames: float32 [65536, 256], P('rows'), may hold values from -0.0625 to 0.0625
Outputs:
- updated_slab: float32 [65536, 4096], P('rows', 'cols')
- projected: float32 [256, 4096], P('rows', 'cols')
The draws below stay inside these ranges and needn't reach their ends.
Inputs may be any that keep to these rules, and one draw needn't show every extreme that they name: `cov_panel`: the rows d1 and d2 restricted to the first 512 columns form a symmetric positive definite matrix.
All inputs are finite; a program needn't handle non-finite values.
Results may differ from the reference program's by a relative error of at most 0.00011.
Values sent between devices are 32-bit elements; how exact they have to be, the bound alone decides.
A program may use at most 64 MiB of HBM per device.

```python
import math
import jax
import jax.numpy as jnp
from jax import lax

PANEL = 256
SLAB = 4096
FRAMES = 256
ROWS_DEV = 1024
GRID = 64
M = 65536
OWN_DEV = 16
N_COLS = 4


def draw_cov_panel(key, part):
    grid_rows = M // ROWS_DEV
    diag_share = PANEL // grid_rows
    full_width = 2 * PANEL
    key_off, key_diag, key_other = jax.random.split(key, 3)
    raw_off = jax.random.normal(key_off, (full_width, full_width), jnp.float32) * (0.5 / math.sqrt(full_width))
    sym_part = (raw_off + raw_off.T) * math.sqrt(0.5)
    sym_part = sym_part * (1.0 - jnp.eye(full_width, dtype=jnp.float32))
    dominance = jax.random.uniform(key_diag, (full_width,), jnp.float32, 1.25, 2.5)
    diag_block = sym_part + jnp.diag(jnp.sum(jnp.abs(sym_part), axis=1) * dominance)
    other_rows = jnp.clip(jax.random.normal(key_other, (grid_rows, ROWS_DEV, full_width), jnp.float32), -6.0, 6.0)
    diag_rows = jnp.concatenate([diag_block[:PANEL].reshape(grid_rows, diag_share, full_width), diag_block[PANEL:].reshape(grid_rows, diag_share, full_width)], axis=1)
    full_rows = jnp.concatenate([diag_rows, other_rows[:, 2 * diag_share:]], axis=1)
    return full_rows.reshape(M, full_width)


def spiked(entries, stream_key, source, target, blocks, factor):
    def block_of(dim):
        return (jnp.arange(entries.shape[dim]) // (entries.shape[dim] // blocks)).reshape((-1,) + (1,) * (entries.ndim - 1 - dim))

    first = jax.random.permutation(stream_key, blocks)[block_of(target)]
    far = (block_of(target) + blocks // 2) % blocks
    return jnp.where((block_of(source) == first) | (block_of(source) == far), factor * entries, entries)


def shard_levels(key, shape, pieces, least, largest):
    gain = 1.0
    for position, blocks in pieces:
        heights = jax.random.uniform(jax.random.fold_in(jax.random.fold_in(key, 6), position), (blocks,), jnp.float32, least / len(pieces), largest / len(pieces))
        gain = gain * jnp.repeat(jnp.exp(heights), shape[position] // blocks).reshape((-1,) + (1,) * (len(shape) - 1 - position))
    return gain


def gaussian(rng, shape, spread, reach, cuts=(), kind=jnp.bfloat16):
    drawn = spread * jax.random.normal(rng, shape, jnp.float32)
    if cuts:
        drawn = drawn * shard_levels(rng, shape, cuts, -0.22, 0.18)
    return jnp.clip(drawn, -reach, reach).astype(kind)


def gaussian_with(rng, dims, spread, bound, shards, heavy, kind=jnp.bfloat16):
    values = spread * jax.random.normal(rng, dims, jnp.float32)
    if shards:
        values = values * shard_levels(rng, dims, shards, -0.22, 0.18)
    return jnp.clip(spiked(values, jax.random.fold_in(rng, 3), *heavy), -bound, bound).astype(kind)


def setup_inputs(seed: int = 0) -> dict:
    seeds = jax.random.split(jax.random.key(seed), 4)
    return {
        "cov_panel": draw_cov_panel(jax.random.fold_in(seeds[3], 71), 0),
        "cov_slab": gaussian(seeds[1], (M, SLAB), 1.0, 6.0, ((0, 64), (1, 4)), jnp.float32),
        "frames": gaussian_with(seeds[2], (M, FRAMES), M ** -0.5, 0.0625, ((0, 64),), (0, 1, 64, 4.0), jnp.float32),
    }


def mat_product(left_op, right_op):
    return jnp.dot(left_op.astype(jnp.float32), right_op.astype(jnp.float32), precision=lax.Precision.HIGHEST, preferred_element_type=jnp.float32)

def right_solve(lower, rhs_rows):
    return lax.linalg.triangular_solve(lower, rhs_rows, left_side=False, lower=True, transpose_a=True)

def reference(cov_panel, cov_slab, frames):
    diag_share = PANEL // GRID
    stacked = cov_panel.reshape(GRID, ROWS_DEV, 2 * PANEL)
    rows_one = stacked[:, :diag_share].reshape(PANEL, 2 * PANEL)
    rows_two = stacked[:, diag_share:2 * diag_share].reshape(PANEL, 2 * PANEL)
    lower_one = jnp.linalg.cholesky(rows_one[:, :PANEL])
    factor_one = right_solve(lower_one, cov_panel[:, :PANEL])
    cross_rows = factor_one.reshape(GRID, ROWS_DEV, PANEL)[:, diag_share:2 * diag_share].reshape(PANEL, PANEL)
    lower_two = jnp.linalg.cholesky(rows_two[:, PANEL:] - mat_product(cross_rows, cross_rows.T))
    factor_two = right_solve(lower_two, cov_panel[:, PANEL:] - mat_product(factor_one, cross_rows.T))
    factor = jnp.concatenate([factor_one, factor_two], axis=1)
    owned = factor.reshape(GRID, ROWS_DEV, 2 * PANEL)[:, 2 * diag_share:2 * diag_share + N_COLS * OWN_DEV]
    owned = owned.reshape(GRID, N_COLS, OWN_DEV, 2 * PANEL).transpose(1, 0, 2, 3).reshape(SLAB, 2 * PANEL)
    updated_slab = cov_slab - mat_product(factor, owned.T)
    projected = mat_product(frames.T, updated_slab)
    return (updated_slab, projected)
```

```python
import functools

import jax
import jax.numpy as jnp
from jax import lax
from jax.experimental import pallas as pl
from jax.experimental.pallas import tpu as pltpu
from jax.sharding import PartitionSpec as P

NZ, NX, NY, NC = 8, 2, 4, 4
NXY = NX * NY
PIV = 16
BLK = 128
MESH = pl.DeviceIdType.MESH
F32, BF16 = jnp.float32, jnp.bfloat16
NN = (((1,), (0,)), ((), ()))
NT = (((1,), (1,)), ((), ()))


def exact(left, right):
    return lax.dot_general(
        left, right, NN, precision=lax.Precision.HIGHEST, preferred_element_type=F32
    )


def halves(x):
    high = x.astype(BF16)
    return high, (x - high.astype(F32)).astype(BF16)


def dot3(left, right, dims):
    (lh, ll), (rh, rl) = left, right
    dot = functools.partial(lax.dot_general, dimension_numbers=dims, preferred_element_type=F32)
    return dot(lh, rh) + (dot(lh, rl) + dot(ll, rh))


def small_inverse(cols):
    row = lax.broadcasted_iota(jnp.int32, (PIV, 128), 0)
    cols = list(cols)
    for j in range(PIV):
        across = [jnp.broadcast_to(col[j : j + 1, :], (PIV, 128)) for col in cols]
        recip = 1.0 / across[j]
        here = row == j
        pivot = jnp.where(here, -1.0, cols[j])
        for k in range(PIV):
            if k != j:
                cols[k] = jnp.where(here, 0.0, cols[k]) - pivot * (across[k] * recip)
        cols[j] = -pivot * recip
    return cols


def block_inverse(parts):
    lane = lax.broadcasted_iota(jnp.int32, (PIV, BLK), 1)
    row = lax.broadcasted_iota(jnp.int32, (PIV, BLK), 0)
    parts = list(parts)
    count = BLK // PIV

    def total(terms):
        sums = terms[:4]
        for i, term in enumerate(terms[4:]):
            sums[i % 4] = sums[i % 4] + term
        return (sums[0] + sums[1]) + (sums[2] + sums[3])

    for m in range(count):
        cols = [
            [
                jnp.broadcast_to(part[:, PIV * m + k : PIV * m + k + 1], (PIV, BLK))
                for k in range(PIV)
            ]
            for part in parts
        ]
        inverse = small_inverse(cols[m])
        inside = (lane >= PIV * m) & (lane < PIV * m + PIV)
        panel = jnp.where(inside, jnp.where(lane - PIV * m == row, 1.0, 0.0), parts[m])
        solved = total(
            [inverse[k] * jnp.broadcast_to(panel[k : k + 1, :], (PIV, BLK)) for k in range(PIV)]
        )
        spread = [jnp.broadcast_to(solved[k : k + 1, :], (PIV, BLK)) for k in range(PIV)]
        for t in range(1, count):
            i = (m + t) % count
            parts[i] = jnp.where(inside, 0.0, parts[i]) - total(
                [cols[i][k] * spread[k] for k in range(PIV)]
            )
        parts[m] = solved
    return jnp.concatenate(parts, axis=0)


def eliminate(mat, k):
    size = mat.shape[0]
    at = pl.multiple_of(k * BLK, BLK)
    parts = [
        mat[pl.ds(pl.multiple_of(at + PIV * i, PIV), PIV), pl.ds(at, BLK)]
        for i in range(BLK // PIV)
    ]
    inverse = block_inverse(parts)
    lane = lax.broadcasted_iota(jnp.int32, (BLK, size), 1) - at
    row = lax.broadcasted_iota(jnp.int32, (BLK, size), 0)
    inside = (lane >= 0) & (lane < BLK)
    panel = jnp.where(inside, jnp.where(lane == row, 1.0, 0.0), mat[pl.ds(at, BLK), :])
    solved = exact(inverse, panel)
    lanes = lax.broadcasted_iota(jnp.int32, (size, size), 1) - at
    cleared = jnp.where((lanes >= 0) & (lanes < BLK), 0.0, mat[...])
    mat[...] = cleared - exact(mat[:, pl.ds(at, BLK)], solved)
    mat[pl.ds(at, BLK), :] = solved


def wait_bytes(ref, sem):
    pltpu.make_async_copy(ref, ref, sem).wait()


def exchange_kernel(
    panel,
    slab,
    frames,
    weights,
    wide,
    proj,
    diag,
    mat,
    owned,
    slab_v,
    frames_v,
    panel_v,
    part,
    part_in,
    line,
    line_in,
    head,
    load_sem,
    send_sem,
    recv_sem,
    ring_send,
    ring_recv,
):
    rows_at, c = lax.axis_index("rows"), lax.axis_index("cols")
    z, xy = rows_at // NXY, lax.rem(rows_at, NXY)
    x, y = xy // NY, lax.rem(xy, NY)

    def place(dz=0, dx=0, dy=0, dc=0):
        z2 = lax.rem(z + dz, NZ)
        x2 = lax.rem(x + dx, NX)
        y2 = lax.rem(y + dy, NY)
        c2 = c
        if dc & 1:
            c2 = c2 + 1 - 2 * lax.rem(c2, 2)
        if dc & 2:
            c2 = lax.rem(c2 + 2, NC)
        return (z2 * NXY + x2 * NY + y2, c2)

    def lanes(col):
        return pl.ds(pl.multiple_of(col * 128, 128), 128)

    def send(src, dst, i, to):
        copy = pltpu.make_async_remote_copy(
            src_ref=src,
            dst_ref=dst,
            send_sem=send_sem.at[i],
            recv_sem=recv_sem.at[i],
            device_id=to,
            device_id_type=MESH,
        )
        copy.start()

    loads = [
        pltpu.make_async_copy(panel, panel_v, load_sem.at[0]),
        pltpu.make_async_copy(frames, frames_v, load_sem.at[1]),
        pltpu.make_async_copy(slab, slab_v, load_sem.at[2]),
        pltpu.make_async_copy(
            panel.at[pl.ds(0, 8), :], diag.at[z, xy, :, lanes(c)], load_sem.at[3]
        ),
        pltpu.make_async_copy(
            panel.at[pl.ds(pl.multiple_of(8 + 16 * c, 8), 16), :],
            owned.at[z, xy, :, lanes(c)],
            load_sem.at[4],
        ),
    ]
    for load in loads:
        load.start()

    line_peers = [dict(dz=d) for d in range(1, NZ)]
    plane_peers = [
        dict(dx=a, dy=b, dc=e) for a in range(NX) for b in range(NY) for e in range(NC) if a or b or e
    ]
    barrier = pltpu.get_barrier_semaphore()
    for peer in line_peers + plane_peers:
        pl.semaphore_signal(barrier, inc=1, device_id=place(**peer), device_id_type=MESH)
    pl.semaphore_wait(barrier, len(line_peers) + len(plane_peers))

    for peer in line_peers:
        send(panel.at[pl.ds(0, 8), :], diag.at[z, xy, :, lanes(c)], 0, place(**peer))
    for e in range(1, NC):
        to = place(dc=e)
        send(
            panel.at[pl.ds(pl.multiple_of(8 + 16 * to[1], 8), 16), :],
            owned.at[z, xy, :, lanes(c)],
            1,
            to,
        )

    loads[0].wait()
    own_wide = pltpu.make_async_copy(panel_v, wide.at[:, lanes(c)], load_sem.at[0])
    own_wide.start()
    loads[1].wait()
    turned = halves(frames_v[...].T)
    shared = dot3(turned, halves(panel_v[...]), NN)
    for g in range(NZ * NXY):
        part[g % NXY, g // NXY, :, 1024:1152] = shared[4 * g : 4 * g + 4, :]
    loads[2].wait()

    def product(i, carry):
        at = pl.multiple_of(i * 256, 256)
        value = dot3(turned, halves(slab_v[:, pl.ds(at, 256)]), NN)
        for g in range(NZ * NXY):
            part[g % NXY, g // NXY, :, pl.ds(at, 256)] = value[4 * g : 4 * g + 4, :]
        return carry

    lax.fori_loop(0, 4, product, 0)

    loads[3].wait()
    wait_bytes(diag.at[pl.ds(0, NZ - 1), xy, :, lanes(c)], recv_sem.at[0])
    same_core = [p for p in plane_peers if not p["dc"] & 1]
    for peer in same_core:
        send(
            diag.at[:, xy, :, lanes(c)], diag.at[:, xy, :, lanes(c)], 2, place(**peer)
        )
    loads[4].wait()
    wait_bytes(owned.at[0, 0, :, pl.ds(0, 384)], recv_sem.at[1])
    plane_only = [p for p in plane_peers if not p["dc"]]
    for peer in plane_only:
        send(owned.at[z, xy], owned.at[z, xy], 3, place(**peer))

    wait_bytes(diag.at[:, pl.ds(0, 5), :, pl.ds(0, 384)], recv_sem.at[2])
    core = lax.rem(c, 2)
    partner = place(dc=1)
    for t in range(2):
        half = diag.at[:, :, :, lanes(core + 2 * t)]
        send(half, half, 4, partner)
    wait_bytes(diag.at[:, :, :, pl.ds(0, 256)], recv_sem.at[4])

    send(panel, wide.at[:, lanes(c)], 5, place(dc=2))
    send(panel, wide.at[:, lanes(c)], 6, partner)
    for peer in plane_only:
        to = place(**peer)
        send(part.at[lax.rem(to[0], NXY)], part_in.at[xy], 7, to)

    def assemble(i, carry):
        zi, q = i // NY, lax.rem(i, NY)
        even, odd = diag[zi, 2 * q], diag[zi, 2 * q + 1]
        first = pl.multiple_of(8 * i, 8)
        mat[pl.ds(first, 8), :] = jnp.concatenate([even[:4], odd[:4]], axis=0)
        mat[pl.ds(pl.multiple_of(256 + first, 8), 8), :] = jnp.concatenate(
            [even[4:], odd[4:]], axis=0
        )
        return carry

    lax.fori_loop(0, NZ * NY, assemble, 0)

    up, down = place(dz=1), place(dz=NZ - 1)

    def block(offset, step, way):
        ref = owned.at[lax.rem(z + offset, NZ)]
        if step == 3:
            ref = ref.at[pl.ds(4 * way, 4)]
        return ref

    def hop(step):
        for way, to in ((0, up), (1, down)):
            off = NZ - step if way == 0 else step
            ref = block(off, step, way)
            pltpu.make_async_remote_copy(
                src_ref=ref,
                dst_ref=ref,
                send_sem=ring_send.at[step, way],
                recv_sem=ring_recv.at[step, way],
                device_id=to,
                device_id_type=MESH,
            ).start()

    def landed(step):
        for way in range(2):
            off = NZ - step - 1 if way == 0 else step + 1
            wait_bytes(block(off, step, way), ring_recv.at[step, way])

    def between(k):
        if k == 0:
            wait_bytes(owned.at[0, pl.ds(0, 7)], recv_sem.at[3])
            hop(0)
        elif k == 1:
            landed(0)
            hop(1)
            wait_bytes(part.at[pl.ds(0, 7)], recv_sem.at[7])
            total = part[xy]
            for i in range(1, NXY):
                total = total + part_in[lax.rem(xy + i, NXY)]
            line[...] = total
            wait_bytes(wide.at[:, pl.ds(0, 128)], recv_sem.at[5])
            far = wide.at[:, lanes(place(dc=2)[1])]
            send(far, far, 8, partner)
        elif k == 2:
            landed(1)
            hop(2)
            for peer in line_peers:
                to = place(**peer)
                send(line.at[to[0] // NXY], line_in.at[z], 9, to)
        else:
            landed(2)
            hop(3)
            wait_bytes(line.at[pl.ds(0, 7)], recv_sem.at[9])
            total = line[z]
            for i in range(1, NZ):
                total = total + line_in[lax.rem(z + i, NZ)]
            proj[...] = total[:, :1024]
            head[c] = total[:, 1024:]

    def step(k, carry):
        eliminate(mat, k)
        for i in range(4):
            pl.when(k == i)(functools.partial(between, i))
        return carry

    lax.fori_loop(0, 4, step, 0)

    landed(3)
    for e in range(1, NC):
        send(head.at[c], head.at[c], 10, place(dc=e))

    inverse = halves(mat[...])

    def weigh(i, carry):
        rows = owned[pl.ds(2 * i, 2)].reshape(256, 512)
        weights[:, pl.ds(pl.multiple_of(i * 256, 256), 256)] = dot3(inverse, halves(rows), NT)
        return carry

    lax.fori_loop(0, 4, weigh, 0)
    wait_bytes(head.at[pl.ds(0, 3)], recv_sem.at[10])
    value = proj[...]
    for e in range(NC):
        value = value - exact(head[e], weights[pl.ds(128 * e, 128), :])
    proj[...] = value

    wait_bytes(wide.at[:, pl.ds(0, 128)], recv_sem.at[6])
    wait_bytes(wide.at[:, pl.ds(0, 128)], recv_sem.at[8])
    own_wide.wait()
    wait_bytes(panel.at[pl.ds(0, 56), :], send_sem.at[0])
    wait_bytes(panel.at[pl.ds(0, 48), :], send_sem.at[1])
    wait_bytes(diag.at[:, pl.ds(0, 5), :, pl.ds(0, 384)], send_sem.at[2])
    wait_bytes(owned.at[0, pl.ds(0, 7)], send_sem.at[3])
    wait_bytes(diag.at[:, :, :, pl.ds(0, 256)], send_sem.at[4])
    for i in (5, 6, 8):
        wait_bytes(wide.at[:, pl.ds(0, 128)], send_sem.at[i])
    wait_bytes(part.at[pl.ds(0, 7)], send_sem.at[7])
    wait_bytes(line.at[pl.ds(0, 7)], send_sem.at[9])
    wait_bytes(head.at[pl.ds(0, 3)], send_sem.at[10])
    for step_at in range(4):
        for way in range(2):
            wait_bytes(block(0, step_at, way), ring_send.at[step_at, way])


def exchange(cov_panel, cov_slab, frames):
    any_space = pl.BlockSpec(memory_space=pl.ANY)
    vmem = pl.BlockSpec(memory_space=pltpu.VMEM)
    return pl.pallas_call(
        exchange_kernel,
        out_shape=(
            jax.ShapeDtypeStruct((512, 1024), F32),
            jax.ShapeDtypeStruct((1024, 512), F32),
            jax.ShapeDtypeStruct((4, 1024), F32),
        ),
        in_specs=[any_space] * 3,
        out_specs=(vmem, any_space, vmem),
        scratch_shapes=[
            pltpu.VMEM((NZ, NXY, 8, 512), F32),
            pltpu.VMEM((512, 512), F32),
            pltpu.VMEM((NZ, NXY, 16, 512), F32),
            pltpu.VMEM((1024, 1024), F32),
            pltpu.VMEM((1024, 256), F32),
            pltpu.VMEM((1024, 128), F32),
            pltpu.VMEM((NXY, NZ, 4, 1152), F32),
            pltpu.VMEM((NXY, NZ, 4, 1152), F32),
            pltpu.VMEM((NZ, 4, 1152), F32),
            pltpu.VMEM((NZ, 4, 1152), F32),
            pltpu.VMEM((NC, 4, 128), F32),
            pltpu.SemaphoreType.DMA((5,)),
            pltpu.SemaphoreType.DMA((11,)),
            pltpu.SemaphoreType.DMA((11,)),
            pltpu.SemaphoreType.DMA((4, 2)),
            pltpu.SemaphoreType.DMA((4, 2)),
        ],
        compiler_params=pltpu.CompilerParams(
            collective_id=0, has_side_effects=True, vmem_limit_bytes=60 << 20
        ),
        name="exchange",
    )(cov_panel, cov_slab, frames)


def update_kernel(slab, wide, weights, out, high, low):
    @pl.when(pl.program_id(0) == 0)
    def _():
        high[...], low[...] = halves(weights[...])

    out[...] = slab[...] - dot3(halves(wide[...]), (high[...], low[...]), NN)


def update(cov_slab, wide, weights):
    rows = 256
    return pl.pallas_call(
        update_kernel,
        out_shape=jax.ShapeDtypeStruct((1024, 1024), F32),
        grid=(1024 // rows,),
        in_specs=[
            pl.BlockSpec((rows, 1024), lambda i: (i, 0)),
            pl.BlockSpec((rows, 512), lambda i: (i, 0)),
            pl.BlockSpec((512, 1024), lambda i: (0, 0), pipeline_mode=pl.Buffered(1)),
        ],
        out_specs=pl.BlockSpec((rows, 1024), lambda i: (i, 0)),
        scratch_shapes=[pltpu.VMEM((512, 1024), BF16), pltpu.VMEM((512, 1024), BF16)],
        compiler_params=pltpu.CompilerParams(vmem_limit_bytes=60 << 20),
        name="update",
    )(cov_slab, wide, weights)


def local(cov_panel, cov_slab, frames):
    weights, wide, projected = exchange(cov_panel, cov_slab, frames)
    return update(cov_slab, wide, weights), projected


def solution(mesh):
    placed = (P("rows", "cols"), P("rows", "cols"), P("rows", None))
    return jax.shard_map(
        local,
        mesh=mesh,
        in_specs=placed,
        out_specs=(P("rows", "cols"), P("rows", "cols")),
        check_vma=False,
    )
```

```python
import functools

import jax
import jax.numpy as jnp
from jax import lax
from jax.experimental import pallas as pl
from jax.experimental.pallas import tpu as pltpu
from jax.sharding import PartitionSpec as P

NZ, NX, NY, NC = 8, 2, 4, 4
NXY = NX * NY
PIV = 16
BLK = 128
MESH = pl.DeviceIdType.MESH
F32, BF16 = jnp.float32, jnp.bfloat16
NN = (((1,), (0,)), ((), ()))
NT = (((1,), (1,)), ((), ()))


def exact(left, right):
    return lax.dot_general(
        left, right, NN, precision=lax.Precision.HIGHEST, preferred_element_type=F32
    )


def halves(x):
    high = x.astype(BF16)
    return high, (x - high.astype(F32)).astype(BF16)


def dot3(left, right, dims):
    (lh, ll), (rh, rl) = left, right
    dot = functools.partial(lax.dot_general, dimension_numbers=dims, preferred_element_type=F32)
    return dot(lh, rh) + (dot(lh, rl) + dot(ll, rh))


def small_inverse(cols):
    row = lax.broadcasted_iota(jnp.int32, (PIV, 128), 0)
    cols = list(cols)
    for j in range(PIV):
        across = [jnp.broadcast_to(col[j : j + 1, :], (PIV, 128)) for col in cols]
        recip = 1.0 / across[j]
        here = row == j
        pivot = jnp.where(here, -1.0, cols[j])
        for k in range(PIV):
            if k != j:
                cols[k] = jnp.where(here, 0.0, cols[k]) - pivot * (across[k] * recip)
        cols[j] = -pivot * recip
    return cols


def block_inverse(parts, midway):
    lane = lax.broadcasted_iota(jnp.int32, (PIV, BLK), 1)
    row = lax.broadcasted_iota(jnp.int32, (PIV, BLK), 0)
    parts = list(parts)
    count = BLK // PIV

    def total(terms):
        sums = terms[:4]
        for i, term in enumerate(terms[4:]):
            sums[i % 4] = sums[i % 4] + term
        return (sums[0] + sums[1]) + (sums[2] + sums[3])

    for m in range(count):
        if m == count // 2:
            midway()
        cols = [
            [
                jnp.broadcast_to(part[:, PIV * m + k : PIV * m + k + 1], (PIV, BLK))
                for k in range(PIV)
            ]
            for part in parts
        ]
        inverse = small_inverse(cols[m])
        inside = (lane >= PIV * m) & (lane < PIV * m + PIV)
        panel = jnp.where(inside, jnp.where(lane - PIV * m == row, 1.0, 0.0), parts[m])
        solved = total(
            [inverse[k] * jnp.broadcast_to(panel[k : k + 1, :], (PIV, BLK)) for k in range(PIV)]
        )
        spread = [jnp.broadcast_to(solved[k : k + 1, :], (PIV, BLK)) for k in range(PIV)]
        for t in range(1, count):
            i = (m + t) % count
            parts[i] = jnp.where(inside, 0.0, parts[i]) - total(
                [cols[i][k] * spread[k] for k in range(PIV)]
            )
        parts[m] = solved
    return jnp.concatenate(parts, axis=0)


def eliminate(mat, k, midway, inverted):
    size = mat.shape[0]
    at = pl.multiple_of(k * BLK, BLK)
    parts = [
        mat[pl.ds(pl.multiple_of(at + PIV * i, PIV), PIV), pl.ds(at, BLK)]
        for i in range(BLK // PIV)
    ]
    inverse = block_inverse(parts, midway)
    inverted()
    lane = lax.broadcasted_iota(jnp.int32, (BLK, size), 1) - at
    row = lax.broadcasted_iota(jnp.int32, (BLK, size), 0)
    inside = (lane >= 0) & (lane < BLK)
    panel = jnp.where(inside, jnp.where(lane == row, 1.0, 0.0), mat[pl.ds(at, BLK), :])
    solved = exact(inverse, panel)
    lanes = lax.broadcasted_iota(jnp.int32, (size, size), 1) - at
    cleared = jnp.where((lanes >= 0) & (lanes < BLK), 0.0, mat[...])
    mat[...] = cleared - exact(mat[:, pl.ds(at, BLK)], solved)
    mat[pl.ds(at, BLK), :] = solved


def wait_bytes(ref, sem):
    pltpu.make_async_copy(ref, ref, sem).wait()


def exchange_kernel(
    panel,
    slab,
    frames,
    high,
    low,
    rows_out,
    wide,
    sums,
    heads,
    diag,
    first,
    mat,
    owned,
    slab_v,
    frames_v,
    panel_v,
    part,
    far_in,
    near_in,
    mid,
    mid_in,
    head,
    load_sem,
    send_sem,
    recv_sem,
    ring_send,
    ring_recv,
    store_sem,
):
    rows_at, c = lax.axis_index("rows"), lax.axis_index("cols")
    z, xy = rows_at // NXY, lax.rem(rows_at, NXY)
    x, y = xy // NY, lax.rem(xy, NY)

    def place(dz=0, dx=0, dy=0, dc=0):
        z2 = lax.rem(z + dz, NZ)
        x2 = lax.rem(x + dx, NX)
        y2 = lax.rem(y + dy, NY)
        c2 = c
        if dc & 1:
            c2 = c2 + 1 - 2 * lax.rem(c2, 2)
        if dc & 2:
            c2 = lax.rem(c2 + 2, NC)
        return (z2 * NXY + x2 * NY + y2, c2)

    def lanes(col):
        return pl.ds(pl.multiple_of(col * 128, 128), 128)

    def send(src, dst, i, to):
        copy = pltpu.make_async_remote_copy(
            src_ref=src,
            dst_ref=dst,
            send_sem=send_sem.at[i],
            recv_sem=recv_sem.at[i],
            device_id=to,
            device_id_type=MESH,
        )
        copy.start()

    loads = [
        pltpu.make_async_copy(panel, panel_v, load_sem.at[0]),
        pltpu.make_async_copy(frames, frames_v, load_sem.at[1]),
        pltpu.make_async_copy(slab, slab_v, load_sem.at[2]),
        pltpu.make_async_copy(
            panel.at[pl.ds(0, 8), :], diag.at[z, xy, :, lanes(c)], load_sem.at[3]
        ),
        pltpu.make_async_copy(
            panel.at[pl.ds(pl.multiple_of(8 + 16 * c, 8), 16), :],
            owned.at[z, xy, :, lanes(c)],
            load_sem.at[4],
        ),
    ]
    for load in loads:
        load.start()

    line_peers = [dict(dz=d) for d in range(1, NZ)]
    plane_peers = [
        dict(dx=a, dy=b, dc=e) for a in range(NX) for b in range(NY) for e in range(NC) if a or b or e
    ]
    barrier = pltpu.get_barrier_semaphore()
    for peer in line_peers + plane_peers:
        pl.semaphore_signal(barrier, inc=1, device_id=place(**peer), device_id_type=MESH)
    pl.semaphore_wait(barrier, len(line_peers) + len(plane_peers))

    for peer in line_peers:
        send(panel.at[pl.ds(0, 8), :], diag.at[z, xy, :, lanes(c)], 0, place(**peer))
    for e in range(1, NC):
        to = place(dc=e)
        send(
            panel.at[pl.ds(pl.multiple_of(8 + 16 * to[1], 8), 16), :],
            owned.at[z, xy, :, lanes(c)],
            1,
            to,
        )

    loads[0].wait()
    own_wide = pltpu.make_async_copy(panel_v, wide.at[:, lanes(c)], load_sem.at[0])
    own_wide.start()
    loads[1].wait()
    turned = halves(frames_v[...].T)

    def keep(value, at, width):
        for g in range(NZ * NXY):
            part[g % NY, g // NY % NX, g // NXY, :, pl.ds(at, width)] = value[4 * g : 4 * g + 4, :]

    keep(dot3(turned, halves(panel_v[...]), NN), 1024, 128)
    loads[2].wait()

    def product(i, carry):
        at = pl.multiple_of(i * 256, 256)
        keep(dot3(turned, halves(slab_v[:, pl.ds(at, 256)]), NN), at, 256)
        return carry

    lax.fori_loop(0, 4, product, 0)

    loads[3].wait()
    wait_bytes(diag.at[pl.ds(0, NZ - 1), xy, :, lanes(c)], recv_sem.at[0])

    @pl.when(c == 0)
    def _():
        for peer in plane_peers:
            send(
                diag.at[pl.ds(0, NZ // 2), xy, :, pl.ds(0, 128)],
                first.at[:, xy],
                14,
                place(**peer),
            )
        pltpu.make_async_copy(
            diag.at[pl.ds(0, NZ // 2), xy, :, pl.ds(0, 128)], first.at[:, xy], load_sem.at[3]
        ).start()

    same_core = [p for p in plane_peers if not p["dc"] & 1]
    for peer in same_core:
        send(diag.at[:, xy, :, lanes(c)], diag.at[:, xy, :, lanes(c)], 2, place(**peer))
    loads[4].wait()
    wait_bytes(owned.at[0, 0, :, pl.ds(0, 384)], recv_sem.at[1])
    plane_only = [p for p in plane_peers if not p["dc"]]
    for peer in plane_only:
        send(owned.at[z, xy], owned.at[z, xy], 3, place(**peer))
    y_next, y_last = lax.rem(y + 1, NY), lax.rem(y + NY - 1, NY)
    y_far = lax.rem(y + 2, NY)
    send(part.at[y_far, 0], far_in.at[0], 7, place(dy=1))
    send(part.at[y_far, 1], far_in.at[1], 9, place(dy=NY - 1))

    core = lax.rem(c, 2)
    partner = place(dc=1)

    def interleave(source, i, width, upper):
        zi, q = i // NY, lax.rem(i, NY)
        even, odd = source[zi, 2 * q], source[zi, 2 * q + 1]
        at = pl.multiple_of(8 * i, 8)
        mat[pl.ds(at, 8), pl.ds(0, width)] = jnp.concatenate([even[:4], odd[:4]], axis=0)
        if upper:
            mat[pl.ds(pl.multiple_of(256 + at, 8), 8), :] = jnp.concatenate(
                [even[4:], odd[4:]], axis=0
            )

    @pl.when(c == 0)
    def _():
        wait_bytes(first.at[:, pl.ds(0, NXY - 1)], recv_sem.at[14])
        wait_bytes(first.at[:, 0], load_sem.at[3])

    @pl.when(c != 0)
    def _():
        wait_bytes(first, recv_sem.at[14])

    def assemble_first(i, carry):
        interleave(first, i, 128, False)
        return carry

    def assemble(i, carry):
        interleave(diag, i, 512, True)
        return carry

    lax.fori_loop(0, NZ // 2 * NY, assemble_first, 0)

    up, down = place(dz=1), place(dz=NZ - 1)

    def block(ref, offset, step, way):
        ref = ref.at[lax.rem(z + offset, NZ)]
        if step == 3:
            ref = ref.at[pl.ds(4 * way, 4)]
        return ref

    def store(step, way, off):
        return pltpu.make_async_copy(
            block(owned, off, step, way), block(rows_out, off, step, way), store_sem.at[step, way]
        )

    def hop(step):
        for way, to in ((0, up), (1, down)):
            ref = block(owned, NZ - step if way == 0 else step, step, way)
            pltpu.make_async_remote_copy(
                src_ref=ref,
                dst_ref=ref,
                send_sem=ring_send.at[step, way],
                recv_sem=ring_recv.at[step, way],
                device_id=to,
                device_id_type=MESH,
            ).start()

    def landed(step):
        for way in range(2):
            off = NZ - step - 1 if way == 0 else step + 1
            wait_bytes(block(owned, off, step, way), ring_recv.at[step, way])
            store(step, way, off).start()

    own_rows = pltpu.make_async_copy(owned.at[z], rows_out.at[z], load_sem.at[4])
    own_head = pltpu.make_async_copy(head, heads.at[c], load_sem.at[1])
    fifteen = part.at[pl.ds(0, 3), 0, pl.ds(0, 5)]
    others = [(a, d) for a in range(NX) for d in range(NZ) if a or d]

    def midway(k):
        if k == 0:
            wait_bytes(diag.at[:, pl.ds(0, 5), :, pl.ds(0, 384)], recv_sem.at[2])
            for t in range(2):
                half = diag.at[:, :, :, lanes(core + 2 * t)]
                send(half, half, 4, partner)
            wait_bytes(far_in.at[0], recv_sem.at[7])
            wait_bytes(far_in.at[1], recv_sem.at[9])
            part[y_next, 0] = part[y_next, 0] + far_in[0]
            part[y_last, 1] = part[y_last, 1] + far_in[1]
            wait_bytes(owned.at[0, pl.ds(0, 7)], recv_sem.at[3])
            hop(0)
            own_rows.start()
            send(part.at[y_next], near_in.at[0], 11, place(dy=1))
            send(part.at[y_last], near_in.at[1], 12, place(dy=NY - 1))
            send(panel, wide.at[:, lanes(c)], 5, place(dc=2))
        elif k == 1:
            landed(0)
            hop(1)
            send(panel, wide.at[:, lanes(c)], 6, partner)
            wait_bytes(near_in.at[0], recv_sem.at[11])
            wait_bytes(near_in.at[1], recv_sem.at[12])
            mid[...] = part[y] + (near_in[0] + near_in[1])
        elif k == 2:
            landed(1)
            hop(2)
            wait_bytes(wide.at[:, pl.ds(0, 128)], recv_sem.at[5])
            far = wide.at[:, lanes(place(dc=2)[1])]
            send(far, far, 8, partner)
        else:
            landed(2)
            hop(3)
            for e in range(1, NC):
                send(head, heads.at[c], 10, place(dc=e))
            own_head.start()

    def inverted(k):
        if k == 0:
            wait_bytes(diag.at[:, :, :, pl.ds(0, 256)], recv_sem.at[4])
            lax.fori_loop(0, NZ * NY, assemble, 0)
        elif k == 1:
            for dx, dz in others:
                to = place(dx=dx, dz=dz)
                zt, xt = to[0] // NXY, lax.rem(to[0], NXY) // NY
                send(mid.at[xt, zt], mid_in.at[x, z], 13, to)
        elif k == 2:
            wait_bytes(fifteen, recv_sem.at[13])
            total = mid[x, z]
            for dx, dz in others:
                total = total + mid_in[lax.rem(x + dx, NX), lax.rem(z + dz, NZ)]
            sums[...] = total[:, :1024]
            head[...] = total[:, 1024:]

    def at_each(k, action, count):
        for i in range(count):
            pl.when(k == i)(functools.partial(action, i))

    def step(k, carry):
        eliminate(
            mat, k, lambda: at_each(k, midway, 4), lambda: at_each(k, inverted, 3)
        )
        return carry

    lax.fori_loop(0, 4, step, 0)

    high[...], low[...] = halves(mat[...])
    landed(3)
    wait_bytes(heads.at[pl.ds(0, 3)], recv_sem.at[10])

    wait_bytes(wide.at[:, pl.ds(0, 128)], recv_sem.at[6])
    wait_bytes(wide.at[:, pl.ds(0, 128)], recv_sem.at[8])
    own_wide.wait()
    own_rows.wait()
    own_head.wait()
    wait_bytes(panel.at[pl.ds(0, 56), :], send_sem.at[0])
    wait_bytes(panel.at[pl.ds(0, 48), :], send_sem.at[1])
    wait_bytes(diag.at[:, pl.ds(0, 5), :, pl.ds(0, 384)], send_sem.at[2])
    wait_bytes(owned.at[0, pl.ds(0, 7)], send_sem.at[3])

    @pl.when(c == 0)
    def _():
        for _ in plane_peers:
            wait_bytes(first.at[:, 0], send_sem.at[14])

    wait_bytes(diag.at[:, :, :, pl.ds(0, 256)], send_sem.at[4])
    for i in (5, 6, 8):
        wait_bytes(wide.at[:, pl.ds(0, 128)], send_sem.at[i])
    for i in (7, 9):
        wait_bytes(far_in.at[0], send_sem.at[i])
    for i in (11, 12):
        wait_bytes(near_in.at[0], send_sem.at[i])
    wait_bytes(heads.at[pl.ds(0, 3)], send_sem.at[10])
    wait_bytes(fifteen, send_sem.at[13])
    for step_at in range(4):
        for way in range(2):
            wait_bytes(block(owned, 0, step_at, way), ring_send.at[step_at, way])
            store(step_at, way, 0).wait()


def exchange(cov_panel, cov_slab, frames):
    any_space = pl.BlockSpec(memory_space=pl.ANY)
    vmem = pl.BlockSpec(memory_space=pltpu.VMEM)
    return pl.pallas_call(
        exchange_kernel,
        out_shape=(
            jax.ShapeDtypeStruct((512, 512), BF16),
            jax.ShapeDtypeStruct((512, 512), BF16),
            jax.ShapeDtypeStruct((NZ, NXY, 16, 512), F32),
            jax.ShapeDtypeStruct((1024, 512), F32),
            jax.ShapeDtypeStruct((4, 1024), F32),
            jax.ShapeDtypeStruct((NC, 4, 128), F32),
        ),
        in_specs=[any_space] * 3,
        out_specs=(vmem, vmem, any_space, any_space, vmem, any_space),
        scratch_shapes=[
            pltpu.VMEM((NZ, NXY, 8, 512), F32),
            pltpu.VMEM((NZ // 2, NXY, 8, 128), F32),
            pltpu.VMEM((512, 512), F32),
            pltpu.VMEM((NZ, NXY, 16, 512), F32),
            pltpu.VMEM((1024, 1024), F32),
            pltpu.VMEM((1024, 256), F32),
            pltpu.VMEM((1024, 128), F32),
            pltpu.VMEM((NY, NX, NZ, 4, 1152), F32),
            pltpu.VMEM((2, NZ, 4, 1152), F32),
            pltpu.VMEM((2, NX, NZ, 4, 1152), F32),
            pltpu.VMEM((NX, NZ, 4, 1152), F32),
            pltpu.VMEM((NX, NZ, 4, 1152), F32),
            pltpu.VMEM((4, 128), F32),
            pltpu.SemaphoreType.DMA((5,)),
            pltpu.SemaphoreType.DMA((15,)),
            pltpu.SemaphoreType.DMA((15,)),
            pltpu.SemaphoreType.DMA((4, 2)),
            pltpu.SemaphoreType.DMA((4, 2)),
            pltpu.SemaphoreType.DMA((4, 2)),
        ],
        compiler_params=pltpu.CompilerParams(
            collective_id=0, has_side_effects=True, vmem_limit_bytes=60 << 20
        ),
        name="exchange",
    )(cov_panel, cov_slab, frames)


COLS = 512


def update_kernel(high, low, rows, wide, slab, sums, heads, out, proj, wide_h, wide_l):
    @pl.when(pl.program_id(0) == 0)
    def _():
        wide_h[...], wide_l[...] = halves(wide[...])

    weights = dot3((high[...], low[...]), halves(rows[...].reshape(COLS, 512)), NT)
    value = sums[...]
    for e in range(NC):
        value = value - exact(heads[e], weights[128 * e : 128 * e + 128, :])
    proj[...] = value
    out[...] = slab[...] - dot3((wide_h[...], wide_l[...]), halves(weights), NN)


def update(high, low, rows, wide, cov_slab, sums, heads):
    once = pl.Buffered(1)
    return pl.pallas_call(
        update_kernel,
        out_shape=(
            jax.ShapeDtypeStruct((1024, 1024), F32),
            jax.ShapeDtypeStruct((4, 1024), F32),
        ),
        grid=(1024 // COLS,),
        in_specs=[
            pl.BlockSpec((512, 512), lambda i: (0, 0), pipeline_mode=once),
            pl.BlockSpec((512, 512), lambda i: (0, 0), pipeline_mode=once),
            pl.BlockSpec((COLS // 128, NXY, 16, 512), lambda i: (i, 0, 0, 0)),
            pl.BlockSpec((1024, 512), lambda i: (0, 0), pipeline_mode=once),
            pl.BlockSpec((1024, COLS), lambda i: (0, i)),
            pl.BlockSpec((4, COLS), lambda i: (0, i)),
            pl.BlockSpec((NC, 4, 128), lambda i: (0, 0, 0), pipeline_mode=once),
        ],
        out_specs=(
            pl.BlockSpec((1024, COLS), lambda i: (0, i)),
            pl.BlockSpec((4, COLS), lambda i: (0, i)),
        ),
        scratch_shapes=[pltpu.VMEM((1024, 512), BF16), pltpu.VMEM((1024, 512), BF16)],
        compiler_params=pltpu.CompilerParams(vmem_limit_bytes=60 << 20),
        name="update",
    )(high, low, rows, wide, cov_slab, sums, heads)


def local(cov_panel, cov_slab, frames):
    high, low, rows, wide, sums, heads = exchange(cov_panel, cov_slab, frames)
    return update(high, low, rows, wide, cov_slab, sums, heads)


def solution(mesh):
    placed = (P("rows", "cols"), P("rows", "cols"), P("rows", None))
    return jax.shard_map(
        local,
        mesh=mesh,
        in_specs=placed,
        out_specs=(P("rows", "cols"), P("rows", "cols")),
        check_vma=False,
    )
```

```python
import functools

import jax
import jax.numpy as jnp
from jax import lax
from jax.experimental import pallas as pl
from jax.experimental.pallas import tpu as pltpu
from jax.sharding import PartitionSpec as P

NZ, NX, NY, NC = 8, 2, 4, 4
NXY = NX * NY
PIV = 16
BLK = 128
MESH = pl.DeviceIdType.MESH
F32, BF16 = jnp.float32, jnp.bfloat16
NN = (((1,), (0,)), ((), ()))
NT = (((1,), (1,)), ((), ()))


def exact(left, right):
    return lax.dot_general(
        left, right, NN, precision=lax.Precision.HIGHEST, preferred_element_type=F32
    )


def halves(x):
    high = x.astype(BF16)
    return high, (x - high.astype(F32)).astype(BF16)


def dot3(left, right, dims):
    (lh, ll), (rh, rl) = left, right
    dot = functools.partial(lax.dot_general, dimension_numbers=dims, preferred_element_type=F32)
    return dot(lh, rh) + (dot(lh, rl) + dot(ll, rh))


def down(rows, k):
    return jnp.broadcast_to(rows[k : k + 1, :], (PIV, 128))


def across(rows, k):
    return jnp.broadcast_to(rows[:, k : k + 1], (PIV, 128))


def total(terms):
    sums = terms[:4]
    for i, term in enumerate(terms[4:]):
        sums[i % 4] = sums[i % 4] + term
    return (sums[0] + sums[1]) + (sums[2] + sums[3])


def small_inverse(cols):
    row = lax.broadcasted_iota(jnp.int32, (PIV, 128), 0)
    cols = list(cols)
    for j in range(0, PIV, 2):
        upper = [down(col, j) for col in cols]
        lower = [down(col, j + 1) for col in cols]
        a, b, d = upper[j], upper[j + 1], lower[j + 1]
        recip = 1.0 / (a * d - b * b)
        inv_a, inv_b, inv_d = d * recip, -(b * recip), a * recip
        first, second = row == j, row == j + 1
        here = first | second
        left = jnp.where(first, -1.0, jnp.where(second, 0.0, cols[j]))
        right = jnp.where(second, -1.0, jnp.where(first, 0.0, cols[j + 1]))
        left, right = left * inv_a + right * inv_b, left * inv_b + right * inv_d
        for k in range(PIV):
            if k not in (j, j + 1):
                cols[k] = jnp.where(here, 0.0, cols[k]) - (left * upper[k] + right * lower[k])
        cols[j], cols[j + 1] = -left, -right
    return cols


def block_inverse(block, midway):
    lane = lax.broadcasted_iota(jnp.int32, (PIV, BLK), 1)
    row = lax.broadcasted_iota(jnp.int32, (PIV, BLK), 0)
    lanes = lax.broadcasted_iota(jnp.int32, (BLK, BLK), 1)
    count = BLK // PIV
    rows = block[0:PIV, :]
    for m in range(count):
        if m == count // 2:
            midway()
        at = PIV * m
        inverse = small_inverse([across(rows, at + k) for k in range(PIV)])
        inside = (lane >= at) & (lane < at + PIV)
        panel = jnp.where(inside, jnp.where(lane - at == row, 1.0, 0.0), rows)
        solved = total([inverse[k] * down(panel, k) for k in range(PIV)])
        if m < count - 1:
            ahead = block[at + PIV : at + 2 * PIV, :]
            rows = jnp.where(inside, 0.0, ahead) - total(
                [across(ahead, at + k) * down(solved, k) for k in range(PIV)]
            )
        whole = block[...]
        cleared = jnp.where((lanes >= at) & (lanes < at + PIV), 0.0, whole)
        block[...] = cleared - exact(whole[:, at : at + PIV], solved)
        block[at : at + PIV, :] = solved
    return block[...]


def eliminate(mat, block, k, midway, inverted):
    size = mat.shape[0]
    at = pl.multiple_of(k * BLK, BLK)
    block[...] = mat[pl.ds(at, BLK), pl.ds(at, BLK)]
    inverse = block_inverse(block, midway)
    inverted()
    lane = lax.broadcasted_iota(jnp.int32, (BLK, size), 1) - at
    row = lax.broadcasted_iota(jnp.int32, (BLK, size), 0)
    inside = (lane >= 0) & (lane < BLK)
    panel = jnp.where(inside, jnp.where(lane == row, 1.0, 0.0), mat[pl.ds(at, BLK), :])
    solved = exact(inverse, panel)
    lanes = lax.broadcasted_iota(jnp.int32, (size, size), 1) - at
    cleared = jnp.where((lanes >= 0) & (lanes < BLK), 0.0, mat[...])
    mat[...] = cleared - exact(mat[:, pl.ds(at, BLK)], solved)
    mat[pl.ds(at, BLK), :] = solved


def wait_bytes(ref, sem):
    pltpu.make_async_copy(ref, ref, sem).wait()


def exchange_kernel(
    panel,
    slab,
    frames,
    high,
    low,
    rows_out,
    wide,
    sums,
    heads,
    diag,
    first,
    mat,
    pivots,
    owned,
    slab_v,
    frames_v,
    panel_v,
    part,
    far_in,
    near_in,
    mid,
    mid_in,
    head,
    load_sem,
    send_sem,
    recv_sem,
    ring_send,
    ring_recv,
    store_sem,
):
    rows_at, c = lax.axis_index("rows"), lax.axis_index("cols")
    z, xy = rows_at // NXY, lax.rem(rows_at, NXY)
    x, y = xy // NY, lax.rem(xy, NY)

    def place(dz=0, dx=0, dy=0, dc=0):
        z2 = lax.rem(z + dz, NZ)
        x2 = lax.rem(x + dx, NX)
        y2 = lax.rem(y + dy, NY)
        c2 = c
        if dc & 1:
            c2 = c2 + 1 - 2 * lax.rem(c2, 2)
        if dc & 2:
            c2 = lax.rem(c2 + 2, NC)
        return (z2 * NXY + x2 * NY + y2, c2)

    def lanes(col):
        return pl.ds(pl.multiple_of(col * 128, 128), 128)

    def send(src, dst, i, to):
        copy = pltpu.make_async_remote_copy(
            src_ref=src,
            dst_ref=dst,
            send_sem=send_sem.at[i],
            recv_sem=recv_sem.at[i],
            device_id=to,
            device_id_type=MESH,
        )
        copy.start()

    loads = [
        pltpu.make_async_copy(panel, panel_v, load_sem.at[0]),
        pltpu.make_async_copy(frames, frames_v, load_sem.at[1]),
        pltpu.make_async_copy(slab, slab_v, load_sem.at[2]),
        pltpu.make_async_copy(
            panel.at[pl.ds(0, 8), :], diag.at[z, xy, :, lanes(c)], load_sem.at[3]
        ),
        pltpu.make_async_copy(
            panel.at[pl.ds(pl.multiple_of(8 + 16 * c, 8), 16), :],
            owned.at[z, xy, :, lanes(c)],
            load_sem.at[4],
        ),
    ]
    for load in loads:
        load.start()

    line_peers = [dict(dz=d) for d in range(1, NZ)]
    plane_peers = [
        dict(dx=a, dy=b, dc=e) for a in range(NX) for b in range(NY) for e in range(NC) if a or b or e
    ]
    barrier = pltpu.get_barrier_semaphore()
    for peer in line_peers + plane_peers:
        pl.semaphore_signal(barrier, inc=1, device_id=place(**peer), device_id_type=MESH)
    pl.semaphore_wait(barrier, len(line_peers) + len(plane_peers))

    for peer in line_peers:
        send(panel.at[pl.ds(0, 8), :], diag.at[z, xy, :, lanes(c)], 0, place(**peer))
    for e in range(1, NC):
        to = place(dc=e)
        send(
            panel.at[pl.ds(pl.multiple_of(8 + 16 * to[1], 8), 16), :],
            owned.at[z, xy, :, lanes(c)],
            1,
            to,
        )

    loads[0].wait()
    own_wide = pltpu.make_async_copy(panel_v, wide.at[:, lanes(c)], load_sem.at[0])
    own_wide.start()
    loads[1].wait()
    turned = halves(frames_v[...].T)

    def keep(value, at, width):
        for g in range(NZ * NXY):
            part[g % NY, g // NY % NX, g // NXY, :, pl.ds(at, width)] = value[4 * g : 4 * g + 4, :]

    keep(dot3(turned, halves(panel_v[...]), NN), 1024, 128)
    loads[2].wait()

    def product(i, carry):
        at = pl.multiple_of(i * 256, 256)
        keep(dot3(turned, halves(slab_v[:, pl.ds(at, 256)]), NN), at, 256)
        return carry

    lax.fori_loop(0, 4, product, 0)

    loads[3].wait()
    wait_bytes(diag.at[pl.ds(0, NZ - 1), xy, :, lanes(c)], recv_sem.at[0])

    @pl.when(c == 0)
    def _():
        for peer in plane_peers:
            send(
                diag.at[pl.ds(0, NZ // 2), xy, :, pl.ds(0, 128)],
                first.at[:, xy],
                14,
                place(**peer),
            )
        pltpu.make_async_copy(
            diag.at[pl.ds(0, NZ // 2), xy, :, pl.ds(0, 128)], first.at[:, xy], load_sem.at[3]
        ).start()

    same_core = [p for p in plane_peers if not p["dc"] & 1]
    for peer in same_core:
        send(diag.at[:, xy, :, lanes(c)], diag.at[:, xy, :, lanes(c)], 2, place(**peer))
    loads[4].wait()
    wait_bytes(owned.at[0, 0, :, pl.ds(0, 384)], recv_sem.at[1])
    plane_only = [p for p in plane_peers if not p["dc"]]
    for peer in plane_only:
        send(owned.at[z, xy], owned.at[z, xy], 3, place(**peer))
    y_next, y_last = lax.rem(y + 1, NY), lax.rem(y + NY - 1, NY)
    y_far = lax.rem(y + 2, NY)
    send(part.at[y_far, 0], far_in.at[0], 7, place(dy=1))
    send(part.at[y_far, 1], far_in.at[1], 9, place(dy=NY - 1))

    core = lax.rem(c, 2)
    partner = place(dc=1)

    def interleave(source, i, width, upper):
        zi, q = i // NY, lax.rem(i, NY)
        even, odd = source[zi, 2 * q], source[zi, 2 * q + 1]
        at = pl.multiple_of(8 * i, 8)
        mat[pl.ds(at, 8), pl.ds(0, width)] = jnp.concatenate([even[:4], odd[:4]], axis=0)
        if upper:
            mat[pl.ds(pl.multiple_of(256 + at, 8), 8), :] = jnp.concatenate(
                [even[4:], odd[4:]], axis=0
            )

    @pl.when(c == 0)
    def _():
        wait_bytes(first.at[:, pl.ds(0, NXY - 1)], recv_sem.at[14])
        wait_bytes(first.at[:, 0], load_sem.at[3])

    @pl.when(c != 0)
    def _():
        wait_bytes(first, recv_sem.at[14])

    def assemble_first(i, carry):
        interleave(first, i, 128, False)
        return carry

    def assemble(i, carry):
        interleave(diag, i, 512, True)
        return carry

    lax.fori_loop(0, NZ // 2 * NY, assemble_first, 0)

    above, below = place(dz=1), place(dz=NZ - 1)

    def block(ref, offset, step, way):
        ref = ref.at[lax.rem(z + offset, NZ)]
        if step == 3:
            ref = ref.at[pl.ds(4 * way, 4)]
        return ref

    def store(step, way, off):
        return pltpu.make_async_copy(
            block(owned, off, step, way), block(rows_out, off, step, way), store_sem.at[step, way]
        )

    def hop(step):
        for way, to in ((0, above), (1, below)):
            ref = block(owned, NZ - step if way == 0 else step, step, way)
            pltpu.make_async_remote_copy(
                src_ref=ref,
                dst_ref=ref,
                send_sem=ring_send.at[step, way],
                recv_sem=ring_recv.at[step, way],
                device_id=to,
                device_id_type=MESH,
            ).start()

    def landed(step):
        for way in range(2):
            off = NZ - step - 1 if way == 0 else step + 1
            wait_bytes(block(owned, off, step, way), ring_recv.at[step, way])
            store(step, way, off).start()

    own_rows = pltpu.make_async_copy(owned.at[z], rows_out.at[z], load_sem.at[4])
    own_head = pltpu.make_async_copy(head, heads.at[c], load_sem.at[1])
    fifteen = part.at[pl.ds(0, 3), 0, pl.ds(0, 5)]
    others = [(a, d) for a in range(NX) for d in range(NZ) if a or d]

    def midway(k):
        if k == 0:
            wait_bytes(diag.at[:, pl.ds(0, 5), :, pl.ds(0, 384)], recv_sem.at[2])
            for t in range(2):
                half = diag.at[:, :, :, lanes(core + 2 * t)]
                send(half, half, 4, partner)
            wait_bytes(far_in.at[0], recv_sem.at[7])
            wait_bytes(far_in.at[1], recv_sem.at[9])
            part[y_next, 0] = part[y_next, 0] + far_in[0]
            part[y_last, 1] = part[y_last, 1] + far_in[1]
            wait_bytes(owned.at[0, pl.ds(0, 7)], recv_sem.at[3])
            hop(0)
            own_rows.start()
            send(part.at[y_next], near_in.at[0], 11, place(dy=1))
            send(part.at[y_last], near_in.at[1], 12, place(dy=NY - 1))
            send(panel, wide.at[:, lanes(c)], 5, place(dc=2))
        elif k == 1:
            landed(0)
            hop(1)
            send(panel, wide.at[:, lanes(c)], 6, partner)
            wait_bytes(near_in.at[0], recv_sem.at[11])
            wait_bytes(near_in.at[1], recv_sem.at[12])
            mid[...] = part[y] + (near_in[0] + near_in[1])
        elif k == 2:
            landed(1)
            hop(2)
            wait_bytes(wide.at[:, pl.ds(0, 128)], recv_sem.at[5])
            far = wide.at[:, lanes(place(dc=2)[1])]
            send(far, far, 8, partner)
        else:
            landed(2)
            hop(3)
            for e in range(1, NC):
                send(head, heads.at[c], 10, place(dc=e))
            own_head.start()

    def inverted(k):
        if k == 0:
            wait_bytes(diag.at[:, :, :, pl.ds(0, 256)], recv_sem.at[4])
            lax.fori_loop(0, NZ * NY, assemble, 0)
        elif k == 1:
            for dx, dz in others:
                to = place(dx=dx, dz=dz)
                zt, xt = to[0] // NXY, lax.rem(to[0], NXY) // NY
                send(mid.at[xt, zt], mid_in.at[x, z], 13, to)
        elif k == 2:
            wait_bytes(fifteen, recv_sem.at[13])
            total = mid[x, z]
            for dx, dz in others:
                total = total + mid_in[lax.rem(x + dx, NX), lax.rem(z + dz, NZ)]
            sums[...] = total[:, :1024]
            head[...] = total[:, 1024:]

    def at_each(k, action, count):
        for i in range(count):
            pl.when(k == i)(functools.partial(action, i))

    def step(k, carry):
        eliminate(
            mat,
            pivots,
            k,
            lambda: at_each(k, midway, 4),
            lambda: at_each(k, inverted, 3),
        )
        return carry

    lax.fori_loop(0, 4, step, 0)

    high[...], low[...] = halves(mat[...])
    landed(3)
    wait_bytes(heads.at[pl.ds(0, 3)], recv_sem.at[10])

    wait_bytes(wide.at[:, pl.ds(0, 128)], recv_sem.at[6])
    wait_bytes(wide.at[:, pl.ds(0, 128)], recv_sem.at[8])
    own_wide.wait()
    own_rows.wait()
    own_head.wait()
    wait_bytes(panel.at[pl.ds(0, 56), :], send_sem.at[0])
    wait_bytes(panel.at[pl.ds(0, 48), :], send_sem.at[1])
    wait_bytes(diag.at[:, pl.ds(0, 5), :, pl.ds(0, 384)], send_sem.at[2])
    wait_bytes(owned.at[0, pl.ds(0, 7)], send_sem.at[3])

    @pl.when(c == 0)
    def _():
        for _ in plane_peers:
            wait_bytes(first.at[:, 0], send_sem.at[14])

    wait_bytes(diag.at[:, :, :, pl.ds(0, 256)], send_sem.at[4])
    for i in (5, 6, 8):
        wait_bytes(wide.at[:, pl.ds(0, 128)], send_sem.at[i])
    for i in (7, 9):
        wait_bytes(far_in.at[0], send_sem.at[i])
    for i in (11, 12):
        wait_bytes(near_in.at[0], send_sem.at[i])
    wait_bytes(heads.at[pl.ds(0, 3)], send_sem.at[10])
    wait_bytes(fifteen, send_sem.at[13])
    for step_at in range(4):
        for way in range(2):
            wait_bytes(block(owned, 0, step_at, way), ring_send.at[step_at, way])
            store(step_at, way, 0).wait()


def exchange(cov_panel, cov_slab, frames):
    any_space = pl.BlockSpec(memory_space=pl.ANY)
    vmem = pl.BlockSpec(memory_space=pltpu.VMEM)
    return pl.pallas_call(
        exchange_kernel,
        out_shape=(
            jax.ShapeDtypeStruct((512, 512), BF16),
            jax.ShapeDtypeStruct((512, 512), BF16),
            jax.ShapeDtypeStruct((NZ, NXY, 16, 512), F32),
            jax.ShapeDtypeStruct((1024, 512), F32),
            jax.ShapeDtypeStruct((4, 1024), F32),
            jax.ShapeDtypeStruct((NC, 4, 128), F32),
        ),
        in_specs=[any_space] * 3,
        out_specs=(vmem, vmem, any_space, any_space, vmem, any_space),
        scratch_shapes=[
            pltpu.VMEM((NZ, NXY, 8, 512), F32),
            pltpu.VMEM((NZ // 2, NXY, 8, 128), F32),
            pltpu.VMEM((512, 512), F32),
            pltpu.VMEM((BLK, BLK), F32),
            pltpu.VMEM((NZ, NXY, 16, 512), F32),
            pltpu.VMEM((1024, 1024), F32),
            pltpu.VMEM((1024, 256), F32),
            pltpu.VMEM((1024, 128), F32),
            pltpu.VMEM((NY, NX, NZ, 4, 1152), F32),
            pltpu.VMEM((2, NZ, 4, 1152), F32),
            pltpu.VMEM((2, NX, NZ, 4, 1152), F32),
            pltpu.VMEM((NX, NZ, 4, 1152), F32),
            pltpu.VMEM((NX, NZ, 4, 1152), F32),
            pltpu.VMEM((4, 128), F32),
            pltpu.SemaphoreType.DMA((5,)),
            pltpu.SemaphoreType.DMA((15,)),
            pltpu.SemaphoreType.DMA((15,)),
            pltpu.SemaphoreType.DMA((4, 2)),
            pltpu.SemaphoreType.DMA((4, 2)),
            pltpu.SemaphoreType.DMA((4, 2)),
        ],
        compiler_params=pltpu.CompilerParams(
            collective_id=0, has_side_effects=True, vmem_limit_bytes=60 << 20
        ),
        name="exchange",
    )(cov_panel, cov_slab, frames)


COLS = 512


def update_kernel(high, low, rows, wide, slab, sums, heads, out, proj, wide_h, wide_l):
    @pl.when(pl.program_id(0) == 0)
    def _():
        wide_h[...], wide_l[...] = halves(wide[...])

    weights = dot3((high[...], low[...]), halves(rows[...].reshape(COLS, 512)), NT)
    value = sums[...]
    for e in range(NC):
        value = value - exact(heads[e], weights[128 * e : 128 * e + 128, :])
    proj[...] = value
    out[...] = slab[...] - dot3((wide_h[...], wide_l[...]), halves(weights), NN)


def update(high, low, rows, wide, cov_slab, sums, heads):
    once = pl.Buffered(1)
    return pl.pallas_call(
        update_kernel,
        out_shape=(
            jax.ShapeDtypeStruct((1024, 1024), F32),
            jax.ShapeDtypeStruct((4, 1024), F32),
        ),
        grid=(1024 // COLS,),
        in_specs=[
            pl.BlockSpec((512, 512), lambda i: (0, 0), pipeline_mode=once),
            pl.BlockSpec((512, 512), lambda i: (0, 0), pipeline_mode=once),
            pl.BlockSpec((COLS // 128, NXY, 16, 512), lambda i: (i, 0, 0, 0)),
            pl.BlockSpec((1024, 512), lambda i: (0, 0), pipeline_mode=once),
            pl.BlockSpec((1024, COLS), lambda i: (0, i)),
            pl.BlockSpec((4, COLS), lambda i: (0, i)),
            pl.BlockSpec((NC, 4, 128), lambda i: (0, 0, 0), pipeline_mode=once),
        ],
        out_specs=(
            pl.BlockSpec((1024, COLS), lambda i: (0, i)),
            pl.BlockSpec((4, COLS), lambda i: (0, i)),
        ),
        scratch_shapes=[pltpu.VMEM((1024, 512), BF16), pltpu.VMEM((1024, 512), BF16)],
        compiler_params=pltpu.CompilerParams(vmem_limit_bytes=60 << 20),
        name="update",
    )(high, low, rows, wide, cov_slab, sums, heads)


def local(cov_panel, cov_slab, frames):
    high, low, rows, wide, sums, heads = exchange(cov_panel, cov_slab, frames)
    return update(high, low, rows, wide, cov_slab, sums, heads)


def solution(mesh):
    placed = (P("rows", "cols"), P("rows", "cols"), P("rows", None))
    return jax.shard_map(
        local,
        mesh=mesh,
        in_specs=placed,
        out_specs=(P("rows", "cols"), P("rows", "cols")),
        check_vma=False,
    )
```

```python
import functools

import jax
import jax.numpy as jnp
from jax import lax
from jax.experimental import pallas as pl
from jax.experimental.pallas import tpu as pltpu
from jax.sharding import PartitionSpec as P

NZ, NX, NY, NC = 8, 2, 4, 4
NXY = NX * NY
PIV = 16
BLK = 128
MESH = pl.DeviceIdType.MESH
F32, BF16 = jnp.float32, jnp.bfloat16
NN = (((1,), (0,)), ((), ()))
NT = (((1,), (1,)), ((), ()))


def exact(left, right):
    return lax.dot_general(
        left, right, NN, precision=lax.Precision.HIGHEST, preferred_element_type=F32
    )


def halves(x):
    high = x.astype(BF16)
    return high, (x - high.astype(F32)).astype(BF16)


def dot3(left, right, dims):
    (lh, ll), (rh, rl) = left, right
    dot = functools.partial(lax.dot_general, dimension_numbers=dims, preferred_element_type=F32)
    return dot(lh, rh) + (dot(lh, rl) + dot(ll, rh))


def down(rows, k):
    return jnp.broadcast_to(rows[k : k + 1, :], (PIV, 128))


def across(rows, k):
    return jnp.broadcast_to(rows[:, k : k + 1], (PIV, 128))


def total(terms):
    sums = terms[:4]
    for i, term in enumerate(terms[4:]):
        sums[i % 4] = sums[i % 4] + term
    return (sums[0] + sums[1]) + (sums[2] + sums[3])


def small_inverse(cols):
    row = lax.broadcasted_iota(jnp.int32, (PIV, 128), 0)
    cols = list(cols)
    for j in range(0, PIV, 2):
        upper = [down(col, j) for col in cols]
        lower = [down(col, j + 1) for col in cols]
        a, b, d = upper[j], upper[j + 1], lower[j + 1]
        recip = 1.0 / (a * d - b * b)
        inv_a, inv_b, inv_d = d * recip, -(b * recip), a * recip
        first, second = row == j, row == j + 1
        here = first | second
        left = jnp.where(first, -1.0, jnp.where(second, 0.0, cols[j]))
        right = jnp.where(second, -1.0, jnp.where(first, 0.0, cols[j + 1]))
        left, right = left * inv_a + right * inv_b, left * inv_b + right * inv_d
        for k in range(PIV):
            if k not in (j, j + 1):
                cols[k] = jnp.where(here, 0.0, cols[k]) - (left * upper[k] + right * lower[k])
        cols[j], cols[j + 1] = -left, -right
    return cols


def block_inverse(block, midway):
    lane = lax.broadcasted_iota(jnp.int32, (PIV, BLK), 1)
    row = lax.broadcasted_iota(jnp.int32, (PIV, BLK), 0)
    lanes = lax.broadcasted_iota(jnp.int32, (BLK, BLK), 1)
    count = BLK // PIV
    rows = block[0:PIV, :]
    for m in range(count):
        if m == count // 2:
            midway()
        at = PIV * m
        inverse = small_inverse([across(rows, at + k) for k in range(PIV)])
        inside = (lane >= at) & (lane < at + PIV)
        panel = jnp.where(inside, jnp.where(lane - at == row, 1.0, 0.0), rows)
        solved = total([inverse[k] * down(panel, k) for k in range(PIV)])
        if m < count - 1:
            ahead = block[at + PIV : at + 2 * PIV, :]
            rows = jnp.where(inside, 0.0, ahead) - total(
                [across(ahead, at + k) * down(solved, k) for k in range(PIV)]
            )
        whole = block[...]
        cleared = jnp.where((lanes >= at) & (lanes < at + PIV), 0.0, whole)
        block[...] = cleared - exact(whole[:, at : at + PIV], solved)
        block[at : at + PIV, :] = solved
    return block[...]


def eliminate(mat, block, k, midway, inverted):
    size = mat.shape[0]
    at = pl.multiple_of(k * BLK, BLK)
    block[...] = mat[pl.ds(at, BLK), pl.ds(at, BLK)]
    inverse = block_inverse(block, midway)
    inverted()
    lane = lax.broadcasted_iota(jnp.int32, (BLK, size), 1) - at
    row = lax.broadcasted_iota(jnp.int32, (BLK, size), 0)
    inside = (lane >= 0) & (lane < BLK)
    panel = jnp.where(inside, jnp.where(lane == row, 1.0, 0.0), mat[pl.ds(at, BLK), :])
    solved = exact(inverse, panel)
    lanes = lax.broadcasted_iota(jnp.int32, (size, size), 1) - at
    cleared = jnp.where((lanes >= 0) & (lanes < BLK), 0.0, mat[...])
    mat[...] = cleared - exact(mat[:, pl.ds(at, BLK)], solved)
    mat[pl.ds(at, BLK), :] = solved


def wait_bytes(ref, sem):
    pltpu.make_async_copy(ref, ref, sem).wait()


def exchange_kernel(
    panel,
    slab,
    frames,
    high,
    low,
    rows_out,
    wide,
    sums,
    heads,
    diag,
    first,
    mat,
    pivots,
    owned,
    slab_v,
    frames_v,
    panel_v,
    part,
    far_in,
    near_in,
    mid,
    mid_in,
    head,
    load_sem,
    send_sem,
    recv_sem,
    ring_send,
    ring_recv,
    store_sem,
):
    rows_at, c = lax.axis_index("rows"), lax.axis_index("cols")
    z, xy = rows_at // NXY, lax.rem(rows_at, NXY)
    x, y = xy // NY, lax.rem(xy, NY)

    def place(dz=0, dx=0, dy=0, dc=0):
        z2 = lax.rem(z + dz, NZ)
        x2 = lax.rem(x + dx, NX)
        y2 = lax.rem(y + dy, NY)
        c2 = c
        if dc & 1:
            c2 = c2 + 1 - 2 * lax.rem(c2, 2)
        if dc & 2:
            c2 = lax.rem(c2 + 2, NC)
        return (z2 * NXY + x2 * NY + y2, c2)

    def lanes(col):
        return pl.ds(pl.multiple_of(col * 128, 128), 128)

    def send(src, dst, i, to):
        copy = pltpu.make_async_remote_copy(
            src_ref=src,
            dst_ref=dst,
            send_sem=send_sem.at[i],
            recv_sem=recv_sem.at[i],
            device_id=to,
            device_id_type=MESH,
        )
        copy.start()

    loads = [
        pltpu.make_async_copy(panel, panel_v, load_sem.at[0]),
        pltpu.make_async_copy(frames, frames_v, load_sem.at[1]),
        pltpu.make_async_copy(slab, slab_v, load_sem.at[2]),
        pltpu.make_async_copy(
            panel.at[pl.ds(0, 8), :], diag.at[z, xy, :, lanes(c)], load_sem.at[3]
        ),
        pltpu.make_async_copy(
            panel.at[pl.ds(pl.multiple_of(8 + 16 * c, 8), 16), :],
            owned.at[z, xy, :, lanes(c)],
            load_sem.at[4],
        ),
    ]
    for load in loads:
        load.start()

    line_peers = [dict(dz=d) for d in range(1, NZ)]
    plane_peers = [
        dict(dx=a, dy=b, dc=e) for a in range(NX) for b in range(NY) for e in range(NC) if a or b or e
    ]
    barrier = pltpu.get_barrier_semaphore()
    for peer in line_peers + plane_peers:
        pl.semaphore_signal(barrier, inc=1, device_id=place(**peer), device_id_type=MESH)
    pl.semaphore_wait(barrier, len(line_peers) + len(plane_peers))

    for peer in line_peers:
        send(panel.at[pl.ds(0, 8), :], diag.at[z, xy, :, lanes(c)], 0, place(**peer))
    for e in range(1, NC):
        to = place(dc=e)
        send(
            panel.at[pl.ds(pl.multiple_of(8 + 16 * to[1], 8), 16), :],
            owned.at[z, xy, :, lanes(c)],
            1,
            to,
        )

    loads[0].wait()
    own_wide = pltpu.make_async_copy(panel_v, wide.at[:, lanes(c)], load_sem.at[0])
    own_wide.start()
    loads[1].wait()
    turned = halves(frames_v[...].T)

    def keep(value, at, width):
        for g in range(NZ * NXY):
            part[g % NY, g // NY % NX, g // NXY, :, pl.ds(at, width)] = value[4 * g : 4 * g + 4, :]

    keep(dot3(turned, halves(panel_v[...]), NN), 1024, 128)
    loads[2].wait()

    def product(i, carry):
        at = pl.multiple_of(i * 256, 256)
        keep(dot3(turned, halves(slab_v[:, pl.ds(at, 256)]), NN), at, 256)
        return carry

    lax.fori_loop(0, 4, product, 0)

    loads[3].wait()
    loads[4].wait()
    wait_bytes(owned.at[0, 0, :, pl.ds(0, 384)], recv_sem.at[1])
    y_next, y_last = lax.rem(y + 1, NY), lax.rem(y + NY - 1, NY)
    y_far = lax.rem(y + 2, NY)
    send(part.at[y_far, 0], far_in.at[0], 7, place(dy=1))
    send(part.at[y_far, 1], far_in.at[1], 9, place(dy=NY - 1))

    wait_bytes(diag.at[pl.ds(0, NZ - 1), xy, :, lanes(c)], recv_sem.at[0])

    @pl.when(c == 0)
    def _():
        for peer in plane_peers:
            send(
                diag.at[pl.ds(0, NZ // 2), xy, :, pl.ds(0, 128)],
                first.at[:, xy],
                14,
                place(**peer),
            )
        pltpu.make_async_copy(
            diag.at[pl.ds(0, NZ // 2), xy, :, pl.ds(0, 128)], first.at[:, xy], load_sem.at[3]
        ).start()

    plane_only = [p for p in plane_peers if not p["dc"]]
    for peer in plane_only:
        send(owned.at[z, xy], owned.at[z, xy], 3, place(**peer))
    same_core = [p for p in plane_peers if not p["dc"] & 1]
    for peer in same_core:
        send(diag.at[:, xy, :, lanes(c)], diag.at[:, xy, :, lanes(c)], 2, place(**peer))
    core = lax.rem(c, 2)
    partner = place(dc=1)

    def interleave(source, i, width, upper):
        zi, q = i // NY, lax.rem(i, NY)
        even, odd = source[zi, 2 * q], source[zi, 2 * q + 1]
        at = pl.multiple_of(8 * i, 8)
        mat[pl.ds(at, 8), pl.ds(0, width)] = jnp.concatenate([even[:4], odd[:4]], axis=0)
        if upper:
            mat[pl.ds(pl.multiple_of(256 + at, 8), 8), :] = jnp.concatenate(
                [even[4:], odd[4:]], axis=0
            )

    above, below = place(dz=1), place(dz=NZ - 1)

    def half(ref, offset, part_at):
        return ref.at[lax.rem(z + offset, NZ), pl.ds(4 * part_at, 4)]

    def ways(step, part_at):
        return ((0, above), (1, below)) if step < 3 else ((part_at, (above, below)[part_at]),)

    def store(step, way, part_at, off):
        return pltpu.make_async_copy(
            half(owned, off, part_at), half(rows_out, off, part_at), store_sem.at[step, way, part_at]
        )

    def hop(step, part_at):
        for way, to in ways(step, part_at):
            ref = half(owned, NZ - step if way == 0 else step, part_at)
            pltpu.make_async_remote_copy(
                src_ref=ref,
                dst_ref=ref,
                send_sem=ring_send.at[step, way, part_at],
                recv_sem=ring_recv.at[step, way, part_at],
                device_id=to,
                device_id_type=MESH,
            ).start()

    def landed(step, part_at):
        for way, _ in ways(step, part_at):
            off = NZ - step - 1 if way == 0 else step + 1
            wait_bytes(half(owned, off, part_at), ring_recv.at[step, way, part_at])
            store(step, way, part_at, off).start()

    def onward(step, part_at):
        landed(step, part_at)
        hop(step + 1, part_at)

    own_rows = pltpu.make_async_copy(owned.at[z], rows_out.at[z], load_sem.at[4])
    own_head = pltpu.make_async_copy(head, heads.at[c], load_sem.at[1])
    fifteen = part.at[pl.ds(0, 3), 0, pl.ds(0, 5)]
    others = [(a, d) for a in range(NX) for d in range(NZ) if a or d]

    wait_bytes(far_in.at[0], recv_sem.at[7])
    wait_bytes(far_in.at[1], recv_sem.at[9])
    part[y_next, 0] = part[y_next, 0] + far_in[0]
    part[y_last, 1] = part[y_last, 1] + far_in[1]
    @pl.when(c == 0)
    def _():
        wait_bytes(first.at[:, pl.ds(0, NXY - 1)], recv_sem.at[14])
        wait_bytes(first.at[:, 0], load_sem.at[3])

    @pl.when(c != 0)
    def _():
        wait_bytes(first, recv_sem.at[14])

    wait_bytes(owned.at[0, pl.ds(0, 7)], recv_sem.at[3])
    hop(0, 0)
    hop(0, 1)
    own_rows.start()

    def assemble_first(i, carry):
        interleave(first, i, 128, False)
        return carry

    def assemble(i, carry):
        interleave(diag, i, 512, True)
        return carry

    lax.fori_loop(0, NZ // 2 * NY, assemble_first, 0)
    send(part.at[y_next], near_in.at[0], 11, place(dy=1))
    send(part.at[y_last], near_in.at[1], 12, place(dy=NY - 1))

    def midway(k):
        if k == 0:
            wait_bytes(diag.at[:, pl.ds(0, 5), :, pl.ds(0, 384)], recv_sem.at[2])
            for t in range(2):
                other = diag.at[:, :, :, lanes(core + 2 * t)]
                send(other, other, 4, partner)
            send(panel, wide.at[:, lanes(c)], 5, place(dc=2))
        elif k == 1:
            wait_bytes(near_in.at[0], recv_sem.at[11])
            wait_bytes(near_in.at[1], recv_sem.at[12])
            mid[...] = part[y] + (near_in[0] + near_in[1])
            onward(0, 1)
            for dx, dz in others:
                to = place(dx=dx, dz=dz)
                zt, xt = to[0] // NXY, lax.rem(to[0], NXY) // NY
                send(mid.at[xt, zt], mid_in.at[x, z], 13, to)
            send(panel, wide.at[:, lanes(c)], 6, partner)
        elif k == 2:
            onward(1, 1)
            wait_bytes(wide.at[:, pl.ds(0, 128)], recv_sem.at[5])
            far = wide.at[:, lanes(place(dc=2)[1])]
            send(far, far, 8, partner)
        else:
            onward(2, 1)
            for e in range(1, NC):
                send(head, heads.at[c], 10, place(dc=e))
            own_head.start()

    def inverted(k):
        if k == 0:
            wait_bytes(diag.at[:, :, :, pl.ds(0, 256)], recv_sem.at[4])
            lax.fori_loop(0, NZ * NY, assemble, 0)
            onward(0, 0)
        elif k == 1:
            onward(1, 0)
        elif k == 2:
            onward(2, 0)
            wait_bytes(fifteen, recv_sem.at[13])
            total = mid[x, z]
            for dx, dz in others:
                total = total + mid_in[lax.rem(x + dx, NX), lax.rem(z + dz, NZ)]
            sums[...] = total[:, :1024]
            head[...] = total[:, 1024:]

    def at_each(k, action, count):
        for i in range(count):
            pl.when(k == i)(functools.partial(action, i))

    def step(k, carry):
        eliminate(
            mat,
            pivots,
            k,
            lambda: at_each(k, midway, 4),
            lambda: at_each(k, inverted, 3),
        )
        return carry

    lax.fori_loop(0, 4, step, 0)

    high[...], low[...] = halves(mat[...])
    landed(3, 0)
    landed(3, 1)
    wait_bytes(heads.at[pl.ds(0, 3)], recv_sem.at[10])

    wait_bytes(wide.at[:, pl.ds(0, 128)], recv_sem.at[6])
    wait_bytes(wide.at[:, pl.ds(0, 128)], recv_sem.at[8])
    own_wide.wait()
    own_rows.wait()
    own_head.wait()
    wait_bytes(panel.at[pl.ds(0, 56), :], send_sem.at[0])
    wait_bytes(panel.at[pl.ds(0, 48), :], send_sem.at[1])
    wait_bytes(diag.at[:, pl.ds(0, 5), :, pl.ds(0, 384)], send_sem.at[2])
    wait_bytes(owned.at[0, pl.ds(0, 7)], send_sem.at[3])

    @pl.when(c == 0)
    def _():
        for _ in plane_peers:
            wait_bytes(first.at[:, 0], send_sem.at[14])

    wait_bytes(diag.at[:, :, :, pl.ds(0, 256)], send_sem.at[4])
    for i in (5, 6, 8):
        wait_bytes(wide.at[:, pl.ds(0, 128)], send_sem.at[i])
    for i in (7, 9):
        wait_bytes(far_in.at[0], send_sem.at[i])
    for i in (11, 12):
        wait_bytes(near_in.at[0], send_sem.at[i])
    wait_bytes(heads.at[pl.ds(0, 3)], send_sem.at[10])
    wait_bytes(fifteen, send_sem.at[13])
    for step_at in range(4):
        for part_at in range(2):
            for way, _ in ways(step_at, part_at):
                wait_bytes(half(owned, 0, part_at), ring_send.at[step_at, way, part_at])
                store(step_at, way, part_at, 0).wait()


def exchange(cov_panel, cov_slab, frames):
    any_space = pl.BlockSpec(memory_space=pl.ANY)
    vmem = pl.BlockSpec(memory_space=pltpu.VMEM)
    return pl.pallas_call(
        exchange_kernel,
        out_shape=(
            jax.ShapeDtypeStruct((512, 512), BF16),
            jax.ShapeDtypeStruct((512, 512), BF16),
            jax.ShapeDtypeStruct((NZ, NXY, 16, 512), F32),
            jax.ShapeDtypeStruct((1024, 512), F32),
            jax.ShapeDtypeStruct((4, 1024), F32),
            jax.ShapeDtypeStruct((NC, 4, 128), F32),
        ),
        in_specs=[any_space] * 3,
        out_specs=(vmem, vmem, any_space, any_space, vmem, any_space),
        scratch_shapes=[
            pltpu.VMEM((NZ, NXY, 8, 512), F32),
            pltpu.VMEM((NZ // 2, NXY, 8, 128), F32),
            pltpu.VMEM((512, 512), F32),
            pltpu.VMEM((BLK, BLK), F32),
            pltpu.VMEM((NZ, NXY, 16, 512), F32),
            pltpu.VMEM((1024, 1024), F32),
            pltpu.VMEM((1024, 256), F32),
            pltpu.VMEM((1024, 128), F32),
            pltpu.VMEM((NY, NX, NZ, 4, 1152), F32),
            pltpu.VMEM((2, NZ, 4, 1152), F32),
            pltpu.VMEM((2, NX, NZ, 4, 1152), F32),
            pltpu.VMEM((NX, NZ, 4, 1152), F32),
            pltpu.VMEM((NX, NZ, 4, 1152), F32),
            pltpu.VMEM((4, 128), F32),
            pltpu.SemaphoreType.DMA((5,)),
            pltpu.SemaphoreType.DMA((15,)),
            pltpu.SemaphoreType.DMA((15,)),
            pltpu.SemaphoreType.DMA((4, 2, 2)),
            pltpu.SemaphoreType.DMA((4, 2, 2)),
            pltpu.SemaphoreType.DMA((4, 2, 2)),
        ],
        compiler_params=pltpu.CompilerParams(
            collective_id=0, has_side_effects=True, vmem_limit_bytes=60 << 20
        ),
        name="exchange",
    )(cov_panel, cov_slab, frames)


COLS = 512


def update_kernel(
    high,
    low,
    rows,
    wide,
    slab,
    sums,
    heads,
    out,
    proj,
    high_v,
    low_v,
    rows_v,
    wide_v,
    slab_v,
    out_v,
    wide_h,
    wide_l,
    sem,
):
    steps = 1024 // COLS
    deep = COLS // 128
    copies = [
        pltpu.make_async_copy(high, high_v, sem.at[0]),
        pltpu.make_async_copy(low, low_v, sem.at[1]),
    ]
    takes = [
        pltpu.make_async_copy(
            rows.at[pl.ds(deep * i, deep)], rows_v.at[pl.ds(deep * i, deep)], sem.at[2 + i]
        )
        for i in range(steps)
    ]
    whole = pltpu.make_async_copy(wide, wide_v, sem.at[2 + steps])
    slabs = [
        pltpu.make_async_copy(
            slab.at[:, pl.ds(COLS * i, COLS)], slab_v.at[:, pl.ds(COLS * i, COLS)], sem.at[4 + steps + i]
        )
        for i in range(steps)
    ]
    gives = [
        pltpu.make_async_copy(
            out_v.at[:, pl.ds(COLS * i, COLS)], out.at[:, pl.ds(COLS * i, COLS)], sem.at[4 + 2 * steps + i]
        )
        for i in range(steps)
    ]
    for copy in copies + takes[:1] + [whole] + slabs[:1] + takes[1:] + slabs[1:]:
        copy.start()
    for copy in copies:
        copy.wait()
    for i in range(steps):
        at = slice(COLS * i, COLS * i + COLS)
        takes[i].wait()
        own = halves(rows_v[deep * i : deep * i + deep].reshape(COLS, 512))
        weights = dot3((high_v[...], low_v[...]), own, NT)
        split = halves(weights)
        across_all = halves(jnp.concatenate([heads[e] for e in range(NC)], axis=1))
        proj[:, at] = sums[:, at] - dot3(across_all, split, NN)
        if i == 0:
            whole.wait()
            wide_h[...], wide_l[...] = halves(wide_v[...])
        slabs[i].wait()
        out_v[:, at] = slab_v[:, at] - dot3((wide_h[...], wide_l[...]), split, NN)
        gives[i].start()
    for copy in gives:
        copy.wait()


def update(high, low, rows, wide, cov_slab, sums, heads):
    any_space = pl.BlockSpec(memory_space=pl.ANY)
    vmem = pl.BlockSpec(memory_space=pltpu.VMEM)
    return pl.pallas_call(
        update_kernel,
        out_shape=(
            jax.ShapeDtypeStruct((1024, 1024), F32),
            jax.ShapeDtypeStruct((4, 1024), F32),
        ),
        in_specs=[any_space] * 5 + [vmem] * 2,
        out_specs=(any_space, vmem),
        scratch_shapes=[
            pltpu.VMEM((512, 512), BF16),
            pltpu.VMEM((512, 512), BF16),
            pltpu.VMEM((NZ, NXY, 16, 512), F32),
            pltpu.VMEM((1024, 512), F32),
            pltpu.VMEM((1024, 1024), F32),
            pltpu.VMEM((1024, 1024), F32),
            pltpu.VMEM((1024, 512), BF16),
            pltpu.VMEM((1024, 512), BF16),
            pltpu.SemaphoreType.DMA((4 + 3 * (1024 // COLS),)),
        ],
        compiler_params=pltpu.CompilerParams(vmem_limit_bytes=60 << 20),
        name="update",
    )(high, low, rows, wide, cov_slab, sums, heads)


def local(cov_panel, cov_slab, frames):
    high, low, rows, wide, sums, heads = exchange(cov_panel, cov_slab, frames)
    return update(high, low, rows, wide, cov_slab, sums, heads)


def solution(mesh):
    placed = (P("rows", "cols"), P("rows", "cols"), P("rows", None))
    return jax.shard_map(
        local,
        mesh=mesh,
        in_specs=placed,
        out_specs=(P("rows", "cols"), P("rows", "cols")),
        check_vma=False,
    )
```

```python
import functools

import jax
import jax.numpy as jnp
from jax import lax
from jax.experimental import pallas as pl
from jax.experimental.pallas import tpu as pltpu
from jax.sharding import PartitionSpec as P

NZ, NX, NY, NC = 8, 2, 4, 4
NXY = NX * NY
PIV = 16
BLK = 128
MESH = pl.DeviceIdType.MESH
F32, BF16 = jnp.float32, jnp.bfloat16
NN = (((1,), (0,)), ((), ()))
NT = (((1,), (1,)), ((), ()))


def exact(left, right):
    return lax.dot_general(
        left, right, NN, precision=lax.Precision.HIGHEST, preferred_element_type=F32
    )


def halves(x):
    high = x.astype(BF16)
    return high, (x - high.astype(F32)).astype(BF16)


def dot3(left, right, dims):
    (lh, ll), (rh, rl) = left, right
    dot = functools.partial(lax.dot_general, dimension_numbers=dims, preferred_element_type=F32)
    return dot(lh, rh) + (dot(lh, rl) + dot(ll, rh))


def down(rows, k):
    return jnp.broadcast_to(rows[k : k + 1, :], (PIV, 128))


def across(rows, k):
    return jnp.broadcast_to(rows[:, k : k + 1], (PIV, 128))


def total(terms):
    sums = terms[:4]
    for i, term in enumerate(terms[4:]):
        sums[i % 4] = sums[i % 4] + term
    return (sums[0] + sums[1]) + (sums[2] + sums[3])


def small_inverse(cols):
    row = lax.broadcasted_iota(jnp.int32, (PIV, 128), 0)
    cols = list(cols)
    for j in range(0, PIV, 2):
        upper = [down(col, j) for col in cols]
        lower = [down(col, j + 1) for col in cols]
        a, b, d = upper[j], upper[j + 1], lower[j + 1]
        recip = 1.0 / (a * d - b * b)
        inv_a, inv_b, inv_d = d * recip, -(b * recip), a * recip
        first, second = row == j, row == j + 1
        here = first | second
        left = jnp.where(first, -1.0, jnp.where(second, 0.0, cols[j]))
        right = jnp.where(second, -1.0, jnp.where(first, 0.0, cols[j + 1]))
        left, right = left * inv_a + right * inv_b, left * inv_b + right * inv_d
        for k in range(PIV):
            if k not in (j, j + 1):
                cols[k] = jnp.where(here, 0.0, cols[k]) - (left * upper[k] + right * lower[k])
        cols[j], cols[j + 1] = -left, -right
    return cols


def block_inverse(block, midway):
    lane = lax.broadcasted_iota(jnp.int32, (PIV, BLK), 1)
    row = lax.broadcasted_iota(jnp.int32, (PIV, BLK), 0)
    lanes = lax.broadcasted_iota(jnp.int32, (BLK, BLK), 1)
    count = BLK // PIV
    rows = block[0:PIV, :]
    for m in range(count):
        if m == count // 2:
            midway()
        at = PIV * m
        inverse = small_inverse([across(rows, at + k) for k in range(PIV)])
        inside = (lane >= at) & (lane < at + PIV)
        panel = jnp.where(inside, jnp.where(lane - at == row, 1.0, 0.0), rows)
        solved = total([inverse[k] * down(panel, k) for k in range(PIV)])
        if m < count - 1:
            ahead = block[at + PIV : at + 2 * PIV, :]
            rows = jnp.where(inside, 0.0, ahead) - total(
                [across(ahead, at + k) * down(solved, k) for k in range(PIV)]
            )
        whole = block[...]
        cleared = jnp.where((lanes >= at) & (lanes < at + PIV), 0.0, whole)
        block[...] = cleared - exact(whole[:, at : at + PIV], solved)
        block[at : at + PIV, :] = solved
    return block[...]


def eliminate(mat, block, k, midway, inverted):
    size = mat.shape[0]
    at = pl.multiple_of(k * BLK, BLK)
    block[...] = mat[pl.ds(at, BLK), pl.ds(at, BLK)]
    inverse = block_inverse(block, midway)
    inverted()
    lane = lax.broadcasted_iota(jnp.int32, (BLK, size), 1) - at
    row = lax.broadcasted_iota(jnp.int32, (BLK, size), 0)
    inside = (lane >= 0) & (lane < BLK)
    panel = jnp.where(inside, jnp.where(lane == row, 1.0, 0.0), mat[pl.ds(at, BLK), :])
    solved = exact(inverse, panel)
    lanes = lax.broadcasted_iota(jnp.int32, (size, size), 1) - at
    cleared = jnp.where((lanes >= 0) & (lanes < BLK), 0.0, mat[...])
    mat[...] = cleared - exact(mat[:, pl.ds(at, BLK)], solved)
    mat[pl.ds(at, BLK), :] = solved


def wait_bytes(ref, sem):
    pltpu.make_async_copy(ref, ref, sem).wait()


def exchange_kernel(
    panel,
    slab,
    frames,
    high,
    low,
    rows_out,
    wide,
    sums,
    heads,
    diag,
    first,
    mat,
    pivots,
    owned,
    slab_v,
    frames_v,
    panel_v,
    part,
    far_in,
    near_in,
    mid,
    mid_in,
    head,
    load_sem,
    send_sem,
    recv_sem,
    ring_send,
    ring_recv,
    store_sem,
):
    rows_at, c = lax.axis_index("rows"), lax.axis_index("cols")
    z, xy = rows_at // NXY, lax.rem(rows_at, NXY)
    x, y = xy // NY, lax.rem(xy, NY)

    def place(dz=0, dx=0, dy=0, dc=0):
        z2 = lax.rem(z + dz, NZ)
        x2 = lax.rem(x + dx, NX)
        y2 = lax.rem(y + dy, NY)
        c2 = c
        if dc & 1:
            c2 = c2 + 1 - 2 * lax.rem(c2, 2)
        if dc & 2:
            c2 = lax.rem(c2 + 2, NC)
        return (z2 * NXY + x2 * NY + y2, c2)

    def lanes(col):
        return pl.ds(pl.multiple_of(col * 128, 128), 128)

    def send(src, dst, i, to):
        copy = pltpu.make_async_remote_copy(
            src_ref=src,
            dst_ref=dst,
            send_sem=send_sem.at[i],
            recv_sem=recv_sem.at[i],
            device_id=to,
            device_id_type=MESH,
        )
        copy.start()

    loads = [
        pltpu.make_async_copy(panel, panel_v, load_sem.at[0]),
        pltpu.make_async_copy(frames, frames_v, load_sem.at[1]),
        pltpu.make_async_copy(slab, slab_v, load_sem.at[2]),
        pltpu.make_async_copy(
            panel.at[pl.ds(0, 8), :], diag.at[z, xy, :, lanes(c)], load_sem.at[3]
        ),
        pltpu.make_async_copy(
            panel.at[pl.ds(pl.multiple_of(8 + 16 * c, 8), 16), :],
            owned.at[z, xy, :, lanes(c)],
            load_sem.at[4],
        ),
    ]
    for load in loads:
        load.start()

    line_peers = [dict(dz=d) for d in range(1, NZ)]
    plane_peers = [
        dict(dx=a, dy=b, dc=e) for a in range(NX) for b in range(NY) for e in range(NC) if a or b or e
    ]
    barrier = pltpu.get_barrier_semaphore()
    for peer in line_peers + plane_peers:
        pl.semaphore_signal(barrier, inc=1, device_id=place(**peer), device_id_type=MESH)
    pl.semaphore_wait(barrier, len(line_peers) + len(plane_peers))

    for peer in line_peers:
        send(panel.at[pl.ds(0, 8), :], diag.at[z, xy, :, lanes(c)], 0, place(**peer))
    for e in range(1, NC):
        to = place(dc=e)
        send(
            panel.at[pl.ds(pl.multiple_of(8 + 16 * to[1], 8), 16), :],
            owned.at[z, xy, :, lanes(c)],
            1,
            to,
        )

    loads[0].wait()
    own_wide = pltpu.make_async_copy(panel_v, wide.at[:, lanes(c)], load_sem.at[0])
    own_wide.start()
    loads[1].wait()
    turned = halves(frames_v[...].T)

    def keep(value, at, width):
        for g in range(NZ * NXY):
            part[g % NY, g // NY % NX, g // NXY, :, pl.ds(at, width)] = value[4 * g : 4 * g + 4, :]

    keep(dot3(turned, halves(panel_v[...]), NN), 1024, 128)
    loads[2].wait()

    def product(i, carry):
        at = pl.multiple_of(i * 256, 256)
        keep(dot3(turned, halves(slab_v[:, pl.ds(at, 256)]), NN), at, 256)
        return carry

    lax.fori_loop(0, 4, product, 0)

    loads[3].wait()
    loads[4].wait()
    wait_bytes(owned.at[0, 0, :, pl.ds(0, 384)], recv_sem.at[1])
    y_next, y_last = lax.rem(y + 1, NY), lax.rem(y + NY - 1, NY)
    y_far = lax.rem(y + 2, NY)
    send(part.at[y_far, 0], far_in.at[0], 7, place(dy=1))
    send(part.at[y_far, 1], far_in.at[1], 9, place(dy=NY - 1))

    wait_bytes(diag.at[pl.ds(0, NZ - 1), xy, :, lanes(c)], recv_sem.at[0])

    @pl.when(c == 0)
    def _():
        for peer in plane_peers:
            send(
                diag.at[pl.ds(0, NZ // 2), xy, :, pl.ds(0, 128)],
                first.at[:, xy],
                14,
                place(**peer),
            )
        pltpu.make_async_copy(
            diag.at[pl.ds(0, NZ // 2), xy, :, pl.ds(0, 128)], first.at[:, xy], load_sem.at[3]
        ).start()

    plane_only = [p for p in plane_peers if not p["dc"]]
    for peer in plane_only:
        send(owned.at[z, xy], owned.at[z, xy], 3, place(**peer))
    same_core = [p for p in plane_peers if not p["dc"] & 1]
    for peer in same_core:
        send(diag.at[:, xy, :, lanes(c)], diag.at[:, xy, :, lanes(c)], 2, place(**peer))
    core = lax.rem(c, 2)
    partner = place(dc=1)

    def interleave(source, i, width, upper):
        zi, q = i // NY, lax.rem(i, NY)
        even, odd = source[zi, 2 * q], source[zi, 2 * q + 1]
        at = pl.multiple_of(8 * i, 8)
        mat[pl.ds(at, 8), pl.ds(0, width)] = jnp.concatenate([even[:4], odd[:4]], axis=0)
        if upper:
            mat[pl.ds(pl.multiple_of(256 + at, 8), 8), :] = jnp.concatenate(
                [even[4:], odd[4:]], axis=0
            )

    above, below = place(dz=1), place(dz=NZ - 1)

    def half(ref, offset, part_at):
        return ref.at[lax.rem(z + offset, NZ), pl.ds(4 * part_at, 4)]

    def ways(step, part_at):
        return ((0, above), (1, below)) if step < 3 else ((part_at, (above, below)[part_at]),)

    def store(step, way, part_at, off):
        return pltpu.make_async_copy(
            half(owned, off, part_at), half(rows_out, off, part_at), store_sem.at[step, way, part_at]
        )

    def hop(step, part_at):
        for way, to in ways(step, part_at):
            ref = half(owned, NZ - step if way == 0 else step, part_at)
            pltpu.make_async_remote_copy(
                src_ref=ref,
                dst_ref=ref,
                send_sem=ring_send.at[step, way, part_at],
                recv_sem=ring_recv.at[step, way, part_at],
                device_id=to,
                device_id_type=MESH,
            ).start()

    def landed(step, part_at):
        for way, _ in ways(step, part_at):
            off = NZ - step - 1 if way == 0 else step + 1
            wait_bytes(half(owned, off, part_at), ring_recv.at[step, way, part_at])
            store(step, way, part_at, off).start()

    def onward(step, part_at):
        landed(step, part_at)
        hop(step + 1, part_at)

    own_rows = pltpu.make_async_copy(owned.at[z], rows_out.at[z], load_sem.at[4])
    own_head = pltpu.make_async_copy(head, heads.at[c], load_sem.at[1])
    fifteen = part.at[pl.ds(0, 3), 0, pl.ds(0, 5)]
    others = [(a, d) for a in range(NX) for d in range(NZ) if a or d]

    wait_bytes(far_in.at[0], recv_sem.at[7])
    wait_bytes(far_in.at[1], recv_sem.at[9])
    part[y_next, 0] = part[y_next, 0] + far_in[0]
    part[y_last, 1] = part[y_last, 1] + far_in[1]
    @pl.when(c == 0)
    def _():
        wait_bytes(first.at[:, pl.ds(0, NXY - 1)], recv_sem.at[14])
        wait_bytes(first.at[:, 0], load_sem.at[3])

    @pl.when(c != 0)
    def _():
        wait_bytes(first, recv_sem.at[14])

    wait_bytes(owned.at[0, pl.ds(0, 7)], recv_sem.at[3])
    hop(0, 0)
    hop(0, 1)
    own_rows.start()

    def assemble_first(i, carry):
        interleave(first, i, 128, False)
        return carry

    def assemble(i, carry):
        interleave(diag, i, 512, True)
        return carry

    lax.fori_loop(0, NZ // 2 * NY, assemble_first, 0)
    send(part.at[y_next], near_in.at[0], 11, place(dy=1))
    send(part.at[y_last], near_in.at[1], 12, place(dy=NY - 1))

    def midway(k):
        if k == 0:
            wait_bytes(diag.at[:, pl.ds(0, 5), :, pl.ds(0, 384)], recv_sem.at[2])
            for t in range(2):
                other = diag.at[:, :, :, lanes(core + 2 * t)]
                send(other, other, 4, partner)
            send(panel, wide.at[:, lanes(c)], 5, place(dc=2))
        elif k == 1:
            wait_bytes(near_in.at[0], recv_sem.at[11])
            wait_bytes(near_in.at[1], recv_sem.at[12])
            mid[...] = part[y] + (near_in[0] + near_in[1])
            onward(0, 1)
            for dx, dz in others:
                to = place(dx=dx, dz=dz)
                zt, xt = to[0] // NXY, lax.rem(to[0], NXY) // NY
                send(mid.at[xt, zt], mid_in.at[x, z], 13, to)
            send(panel, wide.at[:, lanes(c)], 6, partner)
        elif k == 2:
            onward(1, 1)
            wait_bytes(wide.at[:, pl.ds(0, 128)], recv_sem.at[5])
            far = wide.at[:, lanes(place(dc=2)[1])]
            send(far, far, 8, partner)
        else:
            onward(2, 1)
            for e in range(1, NC):
                send(head, heads.at[c], 10, place(dc=e))
            own_head.start()

    def inverted(k):
        if k == 0:
            wait_bytes(diag.at[:, :, :, pl.ds(0, 256)], recv_sem.at[4])
            lax.fori_loop(0, NZ * NY, assemble, 0)
            onward(0, 0)
        elif k == 1:
            onward(1, 0)
        elif k == 2:
            onward(2, 0)
            wait_bytes(fifteen, recv_sem.at[13])
            total = mid[x, z]
            for dx, dz in others:
                total = total + mid_in[lax.rem(x + dx, NX), lax.rem(z + dz, NZ)]
            sums[...] = total[:, :1024]
            head[...] = total[:, 1024:]

    def at_each(k, action, count):
        for i in range(count):
            pl.when(k == i)(functools.partial(action, i))

    def step(k, carry):
        eliminate(
            mat,
            pivots,
            k,
            lambda: at_each(k, midway, 4),
            lambda: at_each(k, inverted, 3),
        )
        return carry

    lax.fori_loop(0, 4, step, 0)

    high[...], low[...] = halves(mat[...])
    landed(3, 0)
    landed(3, 1)
    wait_bytes(heads.at[pl.ds(0, 3)], recv_sem.at[10])

    wait_bytes(wide.at[:, pl.ds(0, 128)], recv_sem.at[6])
    wait_bytes(wide.at[:, pl.ds(0, 128)], recv_sem.at[8])
    own_wide.wait()
    own_rows.wait()
    own_head.wait()
    wait_bytes(panel.at[pl.ds(0, 56), :], send_sem.at[0])
    wait_bytes(panel.at[pl.ds(0, 48), :], send_sem.at[1])
    wait_bytes(diag.at[:, pl.ds(0, 5), :, pl.ds(0, 384)], send_sem.at[2])
    wait_bytes(owned.at[0, pl.ds(0, 7)], send_sem.at[3])

    @pl.when(c == 0)
    def _():
        for _ in plane_peers:
            wait_bytes(first.at[:, 0], send_sem.at[14])

    wait_bytes(diag.at[:, :, :, pl.ds(0, 256)], send_sem.at[4])
    for i in (5, 6, 8):
        wait_bytes(wide.at[:, pl.ds(0, 128)], send_sem.at[i])
    for i in (7, 9):
        wait_bytes(far_in.at[0], send_sem.at[i])
    for i in (11, 12):
        wait_bytes(near_in.at[0], send_sem.at[i])
    wait_bytes(heads.at[pl.ds(0, 3)], send_sem.at[10])
    wait_bytes(fifteen, send_sem.at[13])
    for step_at in range(4):
        for part_at in range(2):
            for way, _ in ways(step_at, part_at):
                wait_bytes(half(owned, 0, part_at), ring_send.at[step_at, way, part_at])
                store(step_at, way, part_at, 0).wait()


def exchange(cov_panel, cov_slab, frames):
    any_space = pl.BlockSpec(memory_space=pl.ANY)
    vmem = pl.BlockSpec(memory_space=pltpu.VMEM)
    return pl.pallas_call(
        exchange_kernel,
        out_shape=(
            jax.ShapeDtypeStruct((512, 512), BF16),
            jax.ShapeDtypeStruct((512, 512), BF16),
            jax.ShapeDtypeStruct((NZ, NXY, 16, 512), F32),
            jax.ShapeDtypeStruct((1024, 512), F32),
            jax.ShapeDtypeStruct((4, 1024), F32),
            jax.ShapeDtypeStruct((NC, 4, 128), F32),
        ),
        in_specs=[any_space] * 3,
        out_specs=(vmem, vmem, any_space, any_space, vmem, any_space),
        scratch_shapes=[
            pltpu.VMEM((NZ, NXY, 8, 512), F32),
            pltpu.VMEM((NZ // 2, NXY, 8, 128), F32),
            pltpu.VMEM((512, 512), F32),
            pltpu.VMEM((BLK, BLK), F32),
            pltpu.VMEM((NZ, NXY, 16, 512), F32),
            pltpu.VMEM((1024, 1024), F32),
            pltpu.VMEM((1024, 256), F32),
            pltpu.VMEM((1024, 128), F32),
            pltpu.VMEM((NY, NX, NZ, 4, 1152), F32),
            pltpu.VMEM((2, NZ, 4, 1152), F32),
            pltpu.VMEM((2, NX, NZ, 4, 1152), F32),
            pltpu.VMEM((NX, NZ, 4, 1152), F32),
            pltpu.VMEM((NX, NZ, 4, 1152), F32),
            pltpu.VMEM((4, 128), F32),
            pltpu.SemaphoreType.DMA((5,)),
            pltpu.SemaphoreType.DMA((15,)),
            pltpu.SemaphoreType.DMA((15,)),
            pltpu.SemaphoreType.DMA((4, 2, 2)),
            pltpu.SemaphoreType.DMA((4, 2, 2)),
            pltpu.SemaphoreType.DMA((4, 2, 2)),
        ],
        compiler_params=pltpu.CompilerParams(
            collective_id=0, has_side_effects=True, vmem_limit_bytes=60 << 20
        ),
        name="exchange",
    )(cov_panel, cov_slab, frames)


COLS = 512


def update_kernel(
    high,
    low,
    rows,
    wide,
    slab,
    sums,
    heads,
    out,
    proj,
    high_v,
    low_v,
    rows_v,
    wide_v,
    slab_v,
    out_v,
    wide_h,
    wide_l,
    sem,
):
    steps = 1024 // COLS
    deep = COLS // 128
    copies = [
        pltpu.make_async_copy(high, high_v, sem.at[0]),
        pltpu.make_async_copy(low, low_v, sem.at[1]),
    ]
    takes = [
        pltpu.make_async_copy(
            rows.at[pl.ds(deep * i, deep)], rows_v.at[pl.ds(deep * i, deep)], sem.at[2 + i]
        )
        for i in range(steps)
    ]
    whole = pltpu.make_async_copy(wide, wide_v, sem.at[2 + steps])
    slabs = [
        pltpu.make_async_copy(
            slab.at[:, pl.ds(COLS * i, COLS)], slab_v.at[:, pl.ds(COLS * i, COLS)], sem.at[4 + steps + i]
        )
        for i in range(steps)
    ]
    gives = [
        pltpu.make_async_copy(
            out_v.at[pl.ds(512 * j, 512), pl.ds(COLS * i, COLS)],
            out.at[pl.ds(512 * j, 512), pl.ds(COLS * i, COLS)],
            sem.at[4 + 2 * steps + 2 * i + j],
        )
        for i in range(steps)
        for j in range(2)
    ]
    for copy in copies + takes[:1] + [whole] + slabs[:1] + takes[1:] + slabs[1:]:
        copy.start()
    for copy in copies:
        copy.wait()
    for i in range(steps):
        at = slice(COLS * i, COLS * i + COLS)
        takes[i].wait()
        own = halves(rows_v[deep * i : deep * i + deep].reshape(COLS, 512))
        weights = dot3((high_v[...], low_v[...]), own, NT)
        split = halves(weights)
        across_all = halves(jnp.concatenate([heads[e] for e in range(NC)], axis=1))
        proj[:, at] = sums[:, at] - dot3(across_all, split, NN)
        if i == 0:
            whole.wait()
            wide_h[...], wide_l[...] = halves(wide_v[...])
        slabs[i].wait()
        for j in range(2):
            up = slice(512 * j, 512 * j + 512)
            out_v[up, at] = slab_v[up, at] - dot3((wide_h[up, :], wide_l[up, :]), split, NN)
            gives[2 * i + j].start()
    for copy in gives:
        copy.wait()


def update(high, low, rows, wide, cov_slab, sums, heads):
    any_space = pl.BlockSpec(memory_space=pl.ANY)
    vmem = pl.BlockSpec(memory_space=pltpu.VMEM)
    return pl.pallas_call(
        update_kernel,
        out_shape=(
            jax.ShapeDtypeStruct((1024, 1024), F32),
            jax.ShapeDtypeStruct((4, 1024), F32),
        ),
        in_specs=[any_space] * 5 + [vmem] * 2,
        out_specs=(any_space, vmem),
        scratch_shapes=[
            pltpu.VMEM((512, 512), BF16),
            pltpu.VMEM((512, 512), BF16),
            pltpu.VMEM((NZ, NXY, 16, 512), F32),
            pltpu.VMEM((1024, 512), F32),
            pltpu.VMEM((1024, 1024), F32),
            pltpu.VMEM((1024, 1024), F32),
            pltpu.VMEM((1024, 512), BF16),
            pltpu.VMEM((1024, 512), BF16),
            pltpu.SemaphoreType.DMA((4 + 4 * (1024 // COLS),)),
        ],
        compiler_params=pltpu.CompilerParams(vmem_limit_bytes=60 << 20),
        name="update",
    )(high, low, rows, wide, cov_slab, sums, heads)


def local(cov_panel, cov_slab, frames):
    high, low, rows, wide, sums, heads = exchange(cov_panel, cov_slab, frames)
    return update(high, low, rows, wide, cov_slab, sums, heads)


def solution(mesh):
    placed = (P("rows", "cols"), P("rows", "cols"), P("rows", None))
    return jax.shard_map(
        local,
        mesh=mesh,
        in_specs=placed,
        out_specs=(P("rows", "cols"), P("rows", "cols")),
        check_vma=False,
    )
```
